128 devices in a mesh: dof: 64 (over z, x, y_hi, core), snap: 2 (over y_lo).
Axes of the slice: x: 4, y: 4 (y_hi: 2, y_lo: 2; y = y_hi * 2 + y_lo), z: 4, core: 2. Of those that a mesh axis runs over, the one named last changes fastest.
Arguments:
- snapshots: float32 [262144, 1024], P('dof', 'snap'), may hold values from -19 to 19
Outputs:
- basis: float32 [262144, 1024], P('dof', 'snap')
- factor: float32 [1024, 1024], P(None, 'snap')
The draws below stay inside these ranges and needn't reach their ends.
All inputs are finite; a program needn't handle non-finite values.
Results may differ from the reference program's by a relative error of at most 0.00024.
Values sent between devices are 32-bit elements; how exact they have to be, the bound alone decides.
A program may use at most 128 MiB of HBM per device.

```python
import math
import jax
import jax.numpy as jnp
from jax import lax

SNAPSHOT_COUNT = 1024
NDOF = 262144


def draw_snapshots(key, part):
    subkeys = jax.random.split(key, 4)
    position = jnp.arange(NDOF, dtype=jnp.float32)[:, None]
    sample_times = jnp.arange(SNAPSHOT_COUNT, dtype=jnp.float32)[None, :]
    angular_rate = jax.random.uniform(subkeys[0], (NDOF, 1), jnp.float32, 0.0, 0.5)
    phase_angles = jax.random.uniform(subkeys[1], (NDOF, 1), jnp.float32, -math.pi, math.pi)
    amplitude = jnp.exp(jax.random.uniform(subkeys[2], (NDOF, 1), jnp.float32, math.log(0.5), math.log(2.0)))
    amplitude = amplitude * (0.6 + 1.2 * position / NDOF)
    rotor_response = 1.2 * jnp.cos(angular_rate * sample_times + phase_angles)
    noises = jnp.clip(jax.random.normal(subkeys[3], (NDOF, SNAPSHOT_COUNT), jnp.float32), -4.0, 4.0)
    return amplitude * (rotor_response + noises)


def setup_inputs(seed: int = 0) -> dict:
    streams_of = jax.random.split(jax.random.key(seed), 2)
    snapshots = draw_snapshots(jax.random.fold_in(streams_of[1], 71), 0)
    return {"snapshots": snapshots}


def reference(snapshots):
    gram = jnp.dot(snapshots.T.astype(jnp.float32), snapshots.astype(jnp.float32), preferred_element_type=jnp.float32, precision=lax.Precision.HIGHEST)
    lower = jnp.linalg.cholesky(gram)
    identity = jnp.eye(SNAPSHOT_COUNT, dtype=jnp.float32)
    inverse = jax.scipy.linalg.solve_triangular(lower, identity, lower=True).T
    root_rows = jnp.sqrt(jnp.float32(NDOF))
    basis = jnp.dot(snapshots.astype(jnp.float32), inverse.astype(jnp.float32), preferred_element_type=jnp.float32, precision=lax.Precision.HIGHEST) * root_rows
    factor = lower.T / root_rows
    return (basis, factor)
```

```python
import functools

import jax
import jax.numpy as jnp
from jax import lax
from jax.experimental import pallas as pl
from jax.experimental.pallas import tpu as pltpu
from jax.sharding import PartitionSpec as P

MESH = pl.DeviceIdType.MESH
HI = lax.Precision.HIGHEST
T = 128

def dot_nt(a, b):
    return lax.dot_general(a, b, (((1,), (1,)), ((), ())), preferred_element_type=jnp.float32, precision=HI)

def dot_nn(a, b):
    return lax.dot_general(a, b, (((1,), (0,)), ((), ())), preferred_element_type=jnp.float32, precision=HI)

def eliminate(block):
    sub = lax.broadcasted_iota(jnp.int32, (8, T), 0)
    lane = lax.broadcasted_iota(jnp.int32, (8, T), 1)
    rows = [block[8 * i:8 * i + 8, :] for i in range(T // 8)]
    upper, lower, pivots = [], [], []
    for b in range(T // 8):
        first = 8 * b
        in_block = (lane >= first) & (lane < first + 8)
        head = rows[b]
        cols = [jnp.broadcast_to(head[:, first + k:first + k + 1], (8, T)) for k in range(8)]
        t = {}
        for k in range(8):
            for j in range(k + 1):
                t[j, k] = jnp.broadcast_to(cols[k][j:j + 1, :], (8, T))
        recip = []
        for j in range(8):
            r = 1.0 / t[j, j]
            recip.append(r)
            for k in range(j + 1, 8):
                s = t[j, k] * r
                for l in range(k, 8):
                    t[k, l] = t[k, l] - s * t[j, l]
        pivot = t[0, 0]
        for j in range(1, 8):
            pivot = jnp.where(sub == j, t[j, j], pivot)
        pivots.append(pivot)

        def multipliers(cs, below):
            cs = list(cs)
            out = []
            for j in range(8):
                m = cs[j] * recip[j]
                if not below:
                    m = jnp.where(sub > j, m, 0.0)
                out.append(m)
                for k in range(j + 1, 8):
                    cs[k] = cs[k] - m * t[j, k]
            return out

        v = jnp.where(in_block, jnp.where(lane == sub + first, 1.0, 0.0), head)
        m = multipliers(cols, False)
        own = head
        for j in range(8):
            v = v - m[j] * jnp.broadcast_to(v[j:j + 1, :], (8, T))
            own = own - m[j] * jnp.broadcast_to(own[j:j + 1, :], (8, T))
        vb = [jnp.broadcast_to(v[j:j + 1, :], (8, T)) for j in range(8)]
        upper.append(jnp.where(lane >= sub + first, own, 0.0))
        lower.append(jnp.where(lane <= sub + first, v, 0.0))
        for i in range(b + 1, T // 8):
            cs = [jnp.broadcast_to(rows[i][:, first + k:first + k + 1], (8, T)) for k in range(8)]
            m = multipliers(cs, True)
            w = jnp.where(in_block, 0.0, rows[i])
            for j in range(8):
                w = w - m[j] * vb[j]
            rows[i] = w
    cat = lambda x: jnp.concatenate(x, axis=0)
    return cat(lower), cat(upper), cat(pivots)

def factor_into(a_ref, l_ref, x_ref, n, lt_ref=None):
    steps = n // T
    def step(p, _):
        at = pl.ds(pl.multiple_of(p * T, T), T)
        low, up, piv = eliminate(a_ref[at, at])
        scale = lax.rsqrt(piv)
        xd = low * scale
        ld = up * scale
        x_ref[at, at] = xd
        l_ref[at, at] = ld.T
        for k in range(steps):
            @pl.when(p == k)
            def _():
                o = k * T
                e = o + T
                if k > 0:
                    part = dot_nn(l_ref[o:e, 0:o], x_ref[0:o, 0:o])
                    x_ref[o:e, 0:o] = -dot_nn(xd, part)
                if e < n:
                    x_ref[o:e, e:n] = jnp.zeros((T, n - e), jnp.float32)
                    l_ref[o:e, e:n] = jnp.zeros((T, n - e), jnp.float32)
                    l21 = dot_nt(a_ref[e:n, o:e], xd)
                    l_ref[e:n, o:e] = l21
                    a_ref[e:n, e:n] = a_ref[e:n, e:n] - dot_nt(l21, l21)
        return 0
    lax.fori_loop(0, steps, step, 0)


VMEM = pl.BlockSpec(memory_space=pltpu.VMEM)


def first_kernel(g_ref, l_ref, x_ref, a_ref):
    a_ref[...] = g_ref[0]
    factor_into(a_ref, l_ref, x_ref, g_ref.shape[1])


def factor_first(grams):
    n = grams.shape[1]
    square = jax.ShapeDtypeStruct((n, n), jnp.float32)
    return pl.pallas_call(
        first_kernel,
        out_shape=(square, square),
        in_specs=[VMEM],
        out_specs=(VMEM, VMEM),
        scratch_shapes=[pltpu.VMEM((n, n), jnp.float32)],
        compiler_params=pltpu.CompilerParams(vmem_limit_bytes=40 << 20),
        cost_estimate=pl.CostEstimate(flops=1 << 30, bytes_accessed=4 << 20, transcendentals=0),
    )(grams)


def second_kernel(g_ref, c_ref, xa_ref, lba_ref, xba_ref, l_ref, x_ref, a_ref):
    n = xa_ref.shape[0]
    lba = dot_nt(c_ref[0], xa_ref[...])
    lba_ref[...] = lba
    a_ref[...] = g_ref[1] - dot_nt(lba, lba)
    factor_into(a_ref, l_ref, x_ref, n)
    xba_ref[...] = -dot_nn(x_ref[...], dot_nn(lba_ref[...], xa_ref[...]))


def factor_second(grams, cross, xa):
    n = xa.shape[0]
    square = jax.ShapeDtypeStruct((n, n), jnp.float32)
    return pl.pallas_call(
        second_kernel,
        out_shape=(square,) * 4,
        in_specs=[VMEM] * 3,
        out_specs=(VMEM,) * 4,
        scratch_shapes=[pltpu.VMEM((n, n), jnp.float32)],
        compiler_params=pltpu.CompilerParams(vmem_limit_bytes=40 << 20),
        cost_estimate=pl.CostEstimate(flops=1 << 30, bytes_accessed=4 << 20, transcendentals=0),
    )(grams, cross, xa)


def reduce_kernel(blocks, p_ref, out_ref, half, quarter, piece, rc, rx, rz, ry, send_sem, recv_sem):
    dof, snap = lax.axis_index("dof"), lax.axis_index("snap")
    core, y_hi = lax.rem(dof, 2), lax.rem(dof // 2, 2)
    x, z = lax.rem(dof // 4, 4), dof // 16
    y = y_hi * 2 + snap

    def device(z, x, y, core):
        return (z * 16 + x * 4 + (y // 2) * 2 + core, lax.rem(y, 2))

    over_core = [device(z, x, y, 1 - core)]
    over_x = [device(z, lax.rem(x + k, 4), y, core) for k in (1, 2, 3)]
    over_z = [device(lax.rem(z + k, 4), x, y, core) for k in (1, 2, 3)]
    over_y = [device(z, x, lax.rem(y + k, 4), core) for k in (1, 2, 3)]

    barrier = pltpu.get_barrier_semaphore()
    partners = over_core + over_x + over_z + over_y
    for partner in partners:
        pl.semaphore_signal(barrier, inc=1, device_id=partner, device_id_type=MESH)
    pl.semaphore_wait(barrier, len(partners))

    used = [0]

    def send(src, dst, to):
        i = used[0]
        used[0] += 1
        copy = pltpu.make_async_remote_copy(
            src_ref=src, dst_ref=dst, send_sem=send_sem.at[i], recv_sem=recv_sem.at[i],
            device_id=to, device_id_type=MESH)
        copy.start()
        return copy

    def wait(copies):
        for copy in copies:
            copy.wait()

    n = p_ref.shape[0]
    h, q, s = n // 2, n // 8, n // 32
    rows = lambda start, size: pl.ds(pl.multiple_of(start, size), size)

    wait([send(p_ref.at[rows((1 - core) * h, h)], rc, over_core[0])])
    half[...] = p_ref[rows(core * h, h), :] + rc[...]
    wait([send(half.at[rows(lax.rem(x + k, 4) * q, q)], rx.at[k - 1], over_x[k - 1]) for k in (1, 2, 3)])
    quarter[...] = (half[rows(x * q, q), :] + rx[1]) + (rx[0] + rx[2])
    wait([send(quarter.at[rows(lax.rem(z + k, 4) * s, s)], rz.at[k - 1], over_z[k - 1]) for k in (1, 2, 3)])
    piece[...] = (quarter[rows(z * s, s), :] + rz[1]) + (rz[0] + rz[2])
    copies = [send(piece, ry.at[y], over_y[k - 1]) for k in (1, 2, 3)]
    ry[y] = piece[...]
    wait(copies)
    base = core * h + x * q
    here = rows(base + z * s, s)
    if blocks == 1:
        out_ref[0, here, :] = (ry[0] + ry[1]) + (ry[2] + ry[3])
    else:
        out_ref[0, here, :] = ry[0] + ry[2]
        out_ref[1, here, :] = ry[1] + ry[3]
    part = out_ref.at[:, here]
    wait([send(part, part, over_z[k - 1]) for k in (1, 2, 3)])
    part = out_ref.at[:, rows(base, q)]
    wait([send(part, part, over_x[k - 1]) for k in (1, 2, 3)])
    part = out_ref.at[:, rows(core * h, h)]
    wait([send(part, part, over_core[0])])


def reduce_all(partial, blocks, collective_id):
    n = partial.shape[0]
    f32 = jnp.float32
    return pl.pallas_call(
        functools.partial(reduce_kernel, blocks),
        out_shape=jax.ShapeDtypeStruct((blocks, n, n), f32),
        in_specs=[VMEM],
        out_specs=VMEM,
        scratch_shapes=[
            pltpu.VMEM((n // 2, n), f32),
            pltpu.VMEM((n // 8, n), f32),
            pltpu.VMEM((n // 32, n), f32),
            pltpu.VMEM((n // 2, n), f32),
            pltpu.VMEM((3, n // 8, n), f32),
            pltpu.VMEM((3, n // 32, n), f32),
            pltpu.VMEM((4, n // 32, n), f32),
            pltpu.SemaphoreType.DMA((17,)),
            pltpu.SemaphoreType.DMA((17,)),
        ],
        compiler_params=pltpu.CompilerParams(
            collective_id=collective_id, has_side_effects=True, vmem_limit_bytes=40 << 20),
        cost_estimate=pl.CostEstimate(flops=1 << 30, bytes_accessed=16 << 20, transcendentals=0),
    )(partial)


def matmul(a, b, over):
    return lax.dot_general(
        a, b, ((over[:1], over[1:]), ((), ())), preferred_element_type=jnp.float32, precision=lax.Precision.HIGH)


def on_device(snapshots):
    count, width = snapshots.shape
    snap = lax.axis_index("snap")
    first = snap == 0
    root_rows = jnp.sqrt(jnp.float32(count * lax.axis_size("dof")))
    mid = count // 2
    given = lax.dynamic_slice_in_dim(snapshots, snap * mid, mid, 0)
    kept = lax.dynamic_slice_in_dim(snapshots, (1 - snap) * mid, mid, 0)
    met = lax.ppermute(given, "snap", [(0, 1), (1, 0)])

    grams = reduce_all(matmul(snapshots, snapshots, (0, 0)), 2, 0)
    la, xa = factor_first(grams)
    met, la = lax.optimization_barrier((met, la))
    rest = lax.ppermute(lax.optimization_barrier((snapshots[mid:], met))[0], "snap", [(0, 1)])

    cross = matmul(kept, met, (0, 0))
    cross = reduce_all(jnp.where(first, cross.T, cross), 1, 1)
    lba, xba, lb, xb = factor_second(grams, cross, xa)

    own = jnp.where(first, xa, xb) * root_rows
    other = jnp.where(first, 0.0, xba) * root_rows
    basis = matmul(snapshots, own, (1, 1)) + matmul(jnp.concatenate([met, rest]), other, (1, 1))
    top = jnp.where(first, la, lba).T
    bottom = jnp.where(first, 0.0, lb).T
    factor = jnp.concatenate([top, bottom]) / root_rows
    return (basis, factor)


def solution(mesh):
    in_specs = (P("dof", "snap"),)
    out_specs = (P("dof", "snap"), P(None, "snap"))
    return jax.shard_map(
        on_device, mesh=mesh, in_specs=in_specs, out_specs=out_specs, check_vma=False
    )
```

```python
import functools

import jax
import jax.numpy as jnp
from jax import lax
from jax.experimental import pallas as pl
from jax.experimental.pallas import tpu as pltpu
from jax.sharding import PartitionSpec as P

MESH = pl.DeviceIdType.MESH
HI = lax.Precision.HIGHEST
T = 128

def dot_nt(a, b):
    return lax.dot_general(a, b, (((1,), (1,)), ((), ())), preferred_element_type=jnp.float32, precision=HI)

def dot_nn(a, b):
    return lax.dot_general(a, b, (((1,), (0,)), ((), ())), preferred_element_type=jnp.float32, precision=HI)

def eliminate(block):
    sub = lax.broadcasted_iota(jnp.int32, (8, T), 0)
    lane = lax.broadcasted_iota(jnp.int32, (8, T), 1)
    rows = [block[8 * i:8 * i + 8, :] for i in range(T // 8)]
    upper, lower, pivots = [], [], []
    for b in range(T // 8):
        first = 8 * b
        in_block = (lane >= first) & (lane < first + 8)
        head = rows[b]
        cols = [jnp.broadcast_to(head[:, first + k:first + k + 1], (8, T)) for k in range(8)]
        t = {}
        for k in range(8):
            for j in range(k + 1):
                t[j, k] = jnp.broadcast_to(cols[k][j:j + 1, :], (8, T))
        recip = []
        for j in range(8):
            r = 1.0 / t[j, j]
            recip.append(r)
            for k in range(j + 1, 8):
                s = t[j, k] * r
                for l in range(k, 8):
                    t[k, l] = t[k, l] - s * t[j, l]
        pivot = t[0, 0]
        for j in range(1, 8):
            pivot = jnp.where(sub == j, t[j, j], pivot)
        pivots.append(pivot)

        def multipliers(cs, below):
            cs = list(cs)
            out = []
            for j in range(8):
                m = cs[j] * recip[j]
                if not below:
                    m = jnp.where(sub > j, m, 0.0)
                out.append(m)
                for k in range(j + 1, 8):
                    cs[k] = cs[k] - m * t[j, k]
            return out

        v = jnp.where(in_block, jnp.where(lane == sub + first, 1.0, 0.0), head)
        m = multipliers(cols, False)
        own = head
        for j in range(8):
            v = v - m[j] * jnp.broadcast_to(v[j:j + 1, :], (8, T))
            own = own - m[j] * jnp.broadcast_to(own[j:j + 1, :], (8, T))
        vb = [jnp.broadcast_to(v[j:j + 1, :], (8, T)) for j in range(8)]
        upper.append(jnp.where(lane >= sub + first, own, 0.0))
        lower.append(jnp.where(lane <= sub + first, v, 0.0))
        for i in range(b + 1, T // 8):
            cs = [jnp.broadcast_to(rows[i][:, first + k:first + k + 1], (8, T)) for k in range(8)]
            m = multipliers(cs, True)
            w = jnp.where(in_block, 0.0, rows[i])
            for j in range(8):
                w = w - m[j] * vb[j]
            rows[i] = w
    cat = lambda x: jnp.concatenate(x, axis=0)
    return cat(lower), cat(upper), cat(pivots)

def factor_into(a_ref, l_ref, x_ref, n, lt_ref=None):
    steps = n // T
    def step(p, _):
        at = pl.ds(pl.multiple_of(p * T, T), T)
        low, up, piv = eliminate(a_ref[at, at])
        scale = lax.rsqrt(piv)
        xd = low * scale
        ld = up * scale
        x_ref[at, at] = xd
        l_ref[at, at] = ld.T
        for k in range(steps):
            @pl.when(p == k)
            def _():
                o = k * T
                e = o + T
                if k > 0:
                    part = dot_nn(l_ref[o:e, 0:o], x_ref[0:o, 0:o])
                    x_ref[o:e, 0:o] = -dot_nn(xd, part)
                if e < n:
                    x_ref[o:e, e:n] = jnp.zeros((T, n - e), jnp.float32)
                    l_ref[o:e, e:n] = jnp.zeros((T, n - e), jnp.float32)
                    l21 = dot_nt(a_ref[e:n, o:e], xd)
                    l_ref[e:n, o:e] = l21
                    a_ref[e:n, e:n] = a_ref[e:n, e:n] - dot_nt(l21, l21)
        return 0
    lax.fori_loop(0, steps, step, 0)


VMEM = pl.BlockSpec(memory_space=pltpu.VMEM)


def first_kernel(g_ref, l_ref, x_ref, a_ref):
    a_ref[...] = g_ref[0]
    factor_into(a_ref, l_ref, x_ref, g_ref.shape[1])


def factor_first(grams):
    n = grams.shape[1]
    square = jax.ShapeDtypeStruct((n, n), jnp.float32)
    return pl.pallas_call(
        first_kernel,
        out_shape=(square, square),
        in_specs=[VMEM],
        out_specs=(VMEM, VMEM),
        scratch_shapes=[pltpu.VMEM((n, n), jnp.float32)],
        compiler_params=pltpu.CompilerParams(vmem_limit_bytes=40 << 20),
        cost_estimate=pl.CostEstimate(flops=24 << 30, bytes_accessed=80 << 20, transcendentals=0),
    )(grams)


def second_kernel(g_ref, c_ref, xa_ref, lba_ref, xba_ref, l_ref, x_ref, a_ref):
    n = xa_ref.shape[0]
    lba = dot_nt(c_ref[0], xa_ref[...])
    lba_ref[...] = lba
    a_ref[...] = g_ref[1] - dot_nt(lba, lba)
    factor_into(a_ref, l_ref, x_ref, n)
    xba_ref[...] = -dot_nn(x_ref[...], dot_nn(lba_ref[...], xa_ref[...]))


def factor_second(grams, cross, xa):
    n = xa.shape[0]
    square = jax.ShapeDtypeStruct((n, n), jnp.float32)
    return pl.pallas_call(
        second_kernel,
        out_shape=(square,) * 4,
        in_specs=[VMEM] * 3,
        out_specs=(VMEM,) * 4,
        scratch_shapes=[pltpu.VMEM((n, n), jnp.float32)],
        compiler_params=pltpu.CompilerParams(vmem_limit_bytes=40 << 20),
        cost_estimate=pl.CostEstimate(flops=24 << 30, bytes_accessed=80 << 20, transcendentals=0),
    )(grams, cross, xa)


def place():
    dof, snap = lax.axis_index("dof"), lax.axis_index("snap")
    core, y_hi = lax.rem(dof, 2), lax.rem(dof // 2, 2)
    return dof // 16, lax.rem(dof // 4, 4), y_hi * 2 + snap, core


def device(z, x, y, core):
    return (z * 16 + x * 4 + (y // 2) * 2 + core, lax.rem(y, 2))


def neighbours(with_y):
    z, x, y, core = place()
    over_core = [device(z, x, y, 1 - core)]
    over_x = [device(z, lax.rem(x + k, 4), y, core) for k in (1, 2, 3)]
    over_z = [device(lax.rem(z + k, 4), x, y, core) for k in (1, 2, 3)]
    down = device(z, x, lax.rem(y + 3, 4), core)
    greet = over_core + over_x + over_z
    if with_y:
        greet = greet + [down, device(z, x, lax.rem(y + 1, 4), core)]
    barrier = pltpu.get_barrier_semaphore()
    for partner in greet:
        pl.semaphore_signal(barrier, inc=1, device_id=partner, device_id_type=MESH)
    pl.semaphore_wait(barrier, len(greet))
    return over_core, over_x, over_z, down


class Sender:
    def __init__(self, send_sem, recv_sem):
        self.sems, self.used = (send_sem, recv_sem), 0

    def start(self, src, dst, to):
        send_sem, recv_sem = (s.at[self.used] for s in self.sems)
        self.used += 1
        copy = pltpu.make_async_remote_copy(
            src_ref=src, dst_ref=dst, send_sem=send_sem, recv_sem=recv_sem, device_id=to, device_id_type=MESH)
        copy.start()
        return copy

    def run(self, triples):
        for copy in [self.start(*t) for t in triples]:
            copy.wait()


def rows(start, size):
    return pl.ds(pl.multiple_of(start, size), size)


def scatter_sum(send, where, p_ref, half, quarter, piece, rc, rx, rz, ry):
    over_core, over_x, over_z, down = where
    z, x, y, core = place()
    n = p_ref.shape[0]
    h, q, s = n // 2, n // 8, n // 32
    send.run([(p_ref.at[rows((1 - core) * h, h)], rc, over_core[0])])
    half[...] = p_ref[rows(core * h, h), :] + rc[...]
    send.run([(half.at[rows(lax.rem(x + k, 4) * q, q)], rx.at[k - 1], over_x[k - 1]) for k in (1, 2, 3)])
    quarter[...] = (half[rows(x * q, q), :] + rx[1]) + (rx[0] + rx[2])
    send.run([(quarter.at[rows(lax.rem(z + k, 4) * s, s)], rz.at[k - 1], over_z[k - 1]) for k in (1, 2, 3)])
    ry[y] = (quarter[rows(z * s, s), :] + rz[1]) + (rz[0] + rz[2])
    for k in (0, 1, 2):
        slot = ry.at[lax.rem(y + k, 4)]
        send.run([(slot, slot, down)])


def gather_rows(send, where, out_ref):
    over_core, over_x, over_z, down = where
    z, x, y, core = place()
    n = out_ref.shape[1]
    h, q, s = n // 2, n // 8, n // 32
    base = core * h + x * q
    part = out_ref.at[:, rows(base + z * s, s)]
    send.run([(part, part, over_z[k - 1]) for k in (1, 2, 3)])
    part = out_ref.at[:, rows(base, q)]
    send.run([(part, part, over_x[k - 1]) for k in (1, 2, 3)])
    part = out_ref.at[:, rows(core * h, h)]
    send.run([(part, part, over_core[0])])


def own_rows(n):
    z, x, y, core = place()
    s = n // 32
    return rows(core * (n // 2) + x * (n // 8) + z * s, s)


def scatter_kernel(p_ref, out_ref, half, quarter, piece, rc, rx, rz, ry, send_sem, recv_sem):
    where = neighbours(True)
    scatter_sum(Sender(send_sem, recv_sem), where, p_ref, half, quarter, piece, rc, rx, rz, ry)
    out_ref[0] = ry[0] + ry[2]
    out_ref[1] = ry[1] + ry[3]


def gather_kernel(p_ref, out_ref, send_sem, recv_sem):
    where = neighbours(False)
    out_ref[:, own_rows(out_ref.shape[1]), :] = p_ref[...]
    gather_rows(Sender(send_sem, recv_sem), where, out_ref)


def reduce_kernel(p_ref, out_ref, half, quarter, piece, rc, rx, rz, ry, send_sem, recv_sem):
    where = neighbours(True)
    send = Sender(send_sem, recv_sem)
    scatter_sum(send, where, p_ref, half, quarter, piece, rc, rx, rz, ry)
    out_ref[0, own_rows(out_ref.shape[1]), :] = (ry[0] + ry[2]) + (ry[1] + ry[3])
    gather_rows(send, where, out_ref)


def scratch(n, copies):
    f32 = jnp.float32
    return [
        pltpu.VMEM((n // 2, n), f32),
        pltpu.VMEM((n // 8, n), f32),
        pltpu.VMEM((n // 32, n), f32),
        pltpu.VMEM((n // 2, n), f32),
        pltpu.VMEM((3, n // 8, n), f32),
        pltpu.VMEM((3, n // 32, n), f32),
        pltpu.VMEM((4, n // 32, n), f32),
        pltpu.SemaphoreType.DMA((copies,)),
        pltpu.SemaphoreType.DMA((copies,)),
    ]


def talk(kernel, out_shape, scratch_shapes, collective_id, operand):
    return pl.pallas_call(
        kernel,
        out_shape=jax.ShapeDtypeStruct(out_shape, jnp.float32),
        in_specs=[VMEM],
        out_specs=VMEM,
        scratch_shapes=scratch_shapes,
        compiler_params=pltpu.CompilerParams(
            collective_id=collective_id, has_side_effects=True, vmem_limit_bytes=40 << 20),
        cost_estimate=pl.CostEstimate(flops=32 << 30, bytes_accessed=100 << 20, transcendentals=0),
    )(operand)


def split(x):
    high = x.astype(jnp.bfloat16)
    return high, (x - high.astype(jnp.float32)).astype(jnp.bfloat16)


def dot3(a, b, over):
    dims = ((over[:1], over[1:]), ((), ()))
    dot = lambda l, r: lax.dot_general(l, r, dims, preferred_element_type=jnp.float32)
    return dot(a[0], b[0]) + (dot(a[0], b[1]) + dot(a[1], b[0]))


CHUNK = 256


def cross_kernel(early, who_ref, own_ref, a_ref, b1_ref, b2_ref, out_ref):
    i = pl.program_id(0)
    second = who_ref[0] == 1
    got = jnp.where(second, a_ref[...], jnp.where(i < early, b1_ref[...], b2_ref[...]))
    own = own_ref[...]
    left = split(jnp.where(second, own, got))
    right = split(jnp.where(second, got, own))

    @pl.when(i == 0)
    def _():
        out_ref[...] = jnp.zeros_like(out_ref)

    out_ref[...] += dot3(left, right, (0, 0))


def cross_gram(snap, own, a, b1, b2):
    steps, n = a.shape[0] // CHUNK, own.shape[1]
    early, late = b1.shape[0] // CHUNK, b2.shape[0] // CHUNK
    block = lambda index: pl.BlockSpec((CHUNK, n), index)
    return pl.pallas_call(
        functools.partial(cross_kernel, early),
        out_shape=jax.ShapeDtypeStruct((n, n), jnp.float32),
        grid_spec=pltpu.PrefetchScalarGridSpec(
            num_scalar_prefetch=1,
            grid=(steps,),
            in_specs=[
                block(lambda i, who: ((1 - who[0]) * steps + i, 0)),
                block(lambda i, who: (who[0] * i, 0)),
                block(lambda i, who: ((1 - who[0]) * jnp.minimum(i, early - 1), 0)),
                block(lambda i, who: ((1 - who[0]) * jnp.clip(i - early, 0, late - 1), 0)),
            ],
            out_specs=pl.BlockSpec((n, n), lambda i, who: (0, 0)),
        ),
        compiler_params=pltpu.CompilerParams(vmem_limit_bytes=40 << 20),
        cost_estimate=pl.CostEstimate(flops=3 << 30, bytes_accessed=12 << 20, transcendentals=0),
    )(snap, own, a, b1, b2)


TALL = 512


def basis_kernel(scale, who_ref, own_ref, a_ref, xa_ref, xb_ref, xba_ref, *others):
    out_ref, high, low, high2, low2 = others[-5:]
    second = who_ref[0] == 1

    @pl.when(pl.program_id(0) == 0)
    def _():
        high[...], low[...] = split(jnp.where(second, xb_ref[...], xa_ref[...]) * scale)
        high2[...], low2[...] = split(xba_ref[...] * scale)

    out_ref[...] = dot3(split(own_ref[...]), (high[...], low[...]), (1, 1))

    @pl.when(second)
    def _():
        out_ref[...] += dot3(split(a_ref[...]), (high2[...], low2[...]), (1, 1))


def basis_rows(scale, first_row, snap, own, a, xa, xb, xba, so_far):
    count, n = own.shape
    steps, offset = a.shape[0] // TALL, first_row // TALL
    whole = pl.BlockSpec((n, n), lambda i, who: (0, 0))
    placed = pl.BlockSpec((TALL, n), lambda i, who: (i + offset, 0))
    extra = [] if so_far is None else [so_far]
    return pl.pallas_call(
        functools.partial(basis_kernel, scale),
        out_shape=jax.ShapeDtypeStruct((count, n), jnp.float32),
        grid_spec=pltpu.PrefetchScalarGridSpec(
            num_scalar_prefetch=1,
            grid=(steps,),
            in_specs=[placed, pl.BlockSpec((TALL, n), lambda i, who: (who[0] * i, 0)), whole, whole, whole]
            + [pl.BlockSpec(memory_space=pl.ANY)] * len(extra),
            out_specs=placed,
            scratch_shapes=[pltpu.VMEM((n, n), jnp.bfloat16)] * 4,
        ),
        input_output_aliases={6: 0} if extra else {},
        compiler_params=pltpu.CompilerParams(vmem_limit_bytes=40 << 20),
        cost_estimate=pl.CostEstimate(flops=6 << 30, bytes_accessed=12 << 20, transcendentals=0),
    )(snap, own, a, xa, xb, xba, *extra)


def on_device(snapshots):
    count, n = snapshots.shape
    snap = lax.axis_index("snap")
    first = snap == 0
    who = snap.astype(jnp.int32).reshape(1)
    rows_in_all = count * lax.axis_size("dof")
    root_rows = float(rows_in_all) ** 0.5
    mid = count // 2
    early = mid + 3 * CHUNK

    tie = lambda *values: lax.optimization_barrier(values)
    a1 = lax.ppermute(snapshots[:mid], "snap", [(0, 1)])
    b1 = lax.ppermute(snapshots[mid:early], "snap", [(1, 0)])
    own_gram = lax.dot_general(
        snapshots, snapshots, (((0,), (0,)), ((), ())), preferred_element_type=jnp.float32, precision=lax.Precision.HIGH)
    pieces = talk(scatter_kernel, (2, n // 32, n), scratch(n, 10), 0, own_gram)
    b1, pieces = tie(b1, pieces)
    late, pieces = tie(snapshots, pieces)
    b2 = lax.ppermute(late[early:], "snap", [(1, 0)])
    a2 = lax.ppermute(late[mid:], "snap", [(0, 1)])
    grams = talk(gather_kernel, (2, n, n), scratch(n, 7)[-2:], 1, pieces)
    la, xa = factor_first(grams)

    a1, b1, b2, la = tie(a1, b1, b2, la)
    cross = cross_gram(who, snapshots, a1, b1, b2)
    cross = talk(reduce_kernel, (1, n, n), scratch(n, 17), 2, cross)
    lba, xba, lb, xb = factor_second(grams, cross, xa)

    basis = basis_rows(root_rows, 0, who, snapshots, a1, xa, xb, xba, None)
    a2, basis = tie(a2, basis)
    basis = basis_rows(root_rows, mid, who, snapshots, a2, xa, xb, xba, basis)
    top = jnp.where(first, la, lba).T
    bottom = jnp.where(first, 0.0, lb).T
    factor = jnp.concatenate([top, bottom]) / root_rows
    return (basis, factor)


def solution(mesh):
    in_specs = (P("dof", "snap"),)
    out_specs = (P("dof", "snap"), P(None, "snap"))
    return jax.shard_map(
        on_device, mesh=mesh, in_specs=in_specs, out_specs=out_specs, check_vma=False
    )
```

```python
import functools

import jax
import jax.numpy as jnp
from jax import lax
from jax.experimental import pallas as pl
from jax.experimental.pallas import tpu as pltpu
from jax.sharding import PartitionSpec as P

MESH = pl.DeviceIdType.MESH
HI = lax.Precision.HIGHEST
T = 128

def dot_nt(a, b):
    return lax.dot_general(a, b, (((1,), (1,)), ((), ())), preferred_element_type=jnp.float32, precision=HI)

def dot_nn(a, b):
    return lax.dot_general(a, b, (((1,), (0,)), ((), ())), preferred_element_type=jnp.float32, precision=HI)

def eliminate(block):
    sub = lax.broadcasted_iota(jnp.int32, (8, T), 0)
    lane = lax.broadcasted_iota(jnp.int32, (8, T), 1)
    rows = [block[8 * i:8 * i + 8, :] for i in range(T // 8)]
    upper, lower, pivots = [], [], []
    for b in range(T // 8):
        first = 8 * b
        in_block = (lane >= first) & (lane < first + 8)
        head = rows[b]
        cols = [jnp.broadcast_to(head[:, first + k:first + k + 1], (8, T)) for k in range(8)]
        t = {}
        for k in range(8):
            for j in range(k + 1):
                t[j, k] = jnp.broadcast_to(cols[k][j:j + 1, :], (8, T))
        recip = []
        for j in range(8):
            r = 1.0 / t[j, j]
            recip.append(r)
            for k in range(j + 1, 8):
                s = t[j, k] * r
                for l in range(k, 8):
                    t[k, l] = t[k, l] - s * t[j, l]
        pivot = t[0, 0]
        for j in range(1, 8):
            pivot = jnp.where(sub == j, t[j, j], pivot)
        pivots.append(pivot)

        def multipliers(cs, below):
            cs = list(cs)
            out = []
            for j in range(8):
                m = cs[j] * recip[j]
                if not below:
                    m = jnp.where(sub > j, m, 0.0)
                out.append(m)
                for k in range(j + 1, 8):
                    cs[k] = cs[k] - m * t[j, k]
            return out

        v = jnp.where(in_block, jnp.where(lane == sub + first, 1.0, 0.0), head)
        m = multipliers(cols, False)
        own = head
        for j in range(8):
            v = v - m[j] * jnp.broadcast_to(v[j:j + 1, :], (8, T))
            own = own - m[j] * jnp.broadcast_to(own[j:j + 1, :], (8, T))
        vb = [jnp.broadcast_to(v[j:j + 1, :], (8, T)) for j in range(8)]
        upper.append(jnp.where(lane >= sub + first, own, 0.0))
        lower.append(jnp.where(lane <= sub + first, v, 0.0))
        for i in range(b + 1, T // 8):
            cs = [jnp.broadcast_to(rows[i][:, first + k:first + k + 1], (8, T)) for k in range(8)]
            m = multipliers(cs, True)
            w = jnp.where(in_block, 0.0, rows[i])
            for j in range(8):
                w = w - m[j] * vb[j]
            rows[i] = w
    cat = lambda x: jnp.concatenate(x, axis=0)
    return cat(lower), cat(upper), cat(pivots)

def factor_into(a_ref, l_ref, x_ref, n, lt_ref=None):
    steps = n // T
    def step(p, _):
        at = pl.ds(pl.multiple_of(p * T, T), T)
        low, up, piv = eliminate(a_ref[at, at])
        scale = lax.rsqrt(piv)
        xd = low * scale
        ld = up * scale
        x_ref[at, at] = xd
        l_ref[at, at] = ld.T
        for k in range(steps):
            @pl.when(p == k)
            def _():
                o = k * T
                e = o + T
                if k > 0:
                    part = dot_nn(l_ref[o:e, 0:o], x_ref[0:o, 0:o])
                    x_ref[o:e, 0:o] = -dot_nn(xd, part)
                if e < n:
                    x_ref[o:e, e:n] = jnp.zeros((T, n - e), jnp.float32)
                    l_ref[o:e, e:n] = jnp.zeros((T, n - e), jnp.float32)
                    l21 = dot_nt(a_ref[e:n, o:e], xd)
                    l_ref[e:n, o:e] = l21
                    a_ref[e:n, e:n] = a_ref[e:n, e:n] - dot_nt(l21, l21)
        return 0
    lax.fori_loop(0, steps, step, 0)


VMEM = pl.BlockSpec(memory_space=pltpu.VMEM)


def second_kernel(g_ref, c_ref, xa_ref, lba_ref, xba_ref, l_ref, x_ref, a_ref):
    n = xa_ref.shape[0]
    lba = dot_nt(c_ref[0], xa_ref[...])
    lba_ref[...] = lba
    a_ref[...] = g_ref[1] - dot_nt(lba, lba)
    factor_into(a_ref, l_ref, x_ref, n)
    xba_ref[...] = -dot_nn(x_ref[...], dot_nn(lba_ref[...], xa_ref[...]))


def factor_second(grams, cross, xa):
    n = xa.shape[0]
    square = jax.ShapeDtypeStruct((n, n), jnp.float32)
    return pl.pallas_call(
        second_kernel,
        out_shape=(square,) * 4,
        in_specs=[VMEM] * 3,
        out_specs=(VMEM,) * 4,
        scratch_shapes=[pltpu.VMEM((n, n), jnp.float32)],
        compiler_params=pltpu.CompilerParams(vmem_limit_bytes=40 << 20),
        cost_estimate=pl.CostEstimate(flops=24 << 30, bytes_accessed=80 << 20, transcendentals=0),
    )(grams, cross, xa)


def place():
    dof, snap = lax.axis_index("dof"), lax.axis_index("snap")
    core, y_hi = lax.rem(dof, 2), lax.rem(dof // 2, 2)
    return dof // 16, lax.rem(dof // 4, 4), y_hi * 2 + snap, core


def device(z, x, y, core):
    return (z * 16 + x * 4 + (y // 2) * 2 + core, lax.rem(y, 2))


def neighbours(with_y):
    z, x, y, core = place()
    over_core = [device(z, x, y, 1 - core)]
    over_x = [device(z, lax.rem(x + k, 4), y, core) for k in (1, 2, 3)]
    over_z = [device(lax.rem(z + k, 4), x, y, core) for k in (1, 2, 3)]
    down = device(z, x, lax.rem(y + 3, 4), core)
    greet = over_core + over_x + over_z
    if with_y:
        greet = greet + [down, device(z, x, lax.rem(y + 1, 4), core)]
    barrier = pltpu.get_barrier_semaphore()
    for partner in greet:
        pl.semaphore_signal(barrier, inc=1, device_id=partner, device_id_type=MESH)
    pl.semaphore_wait(barrier, len(greet))
    return over_core, over_x, over_z, down


class Sender:
    def __init__(self, send_sem, recv_sem):
        self.sems, self.used = (send_sem, recv_sem), 0

    def start(self, src, dst, to):
        send_sem, recv_sem = (s.at[self.used] for s in self.sems)
        self.used += 1
        copy = pltpu.make_async_remote_copy(
            src_ref=src, dst_ref=dst, send_sem=send_sem, recv_sem=recv_sem, device_id=to, device_id_type=MESH)
        copy.start()
        return copy

    def run(self, triples):
        for copy in [self.start(*t) for t in triples]:
            copy.wait()


def rows(start, size):
    return pl.ds(pl.multiple_of(start, size), size)


def scatter_sum(send, where, p_ref, half, quarter, rc, rx, rz, ry):
    over_core, over_x, over_z, down = where
    z, x, y, core = place()
    n = p_ref.shape[0]
    h, q, s = n // 2, n // 8, n // 32
    send.run([(p_ref.at[rows((1 - core) * h, h)], rc, over_core[0])])
    half[...] = p_ref[rows(core * h, h), :] + rc[...]
    send.run([(half.at[rows(lax.rem(x + k, 4) * q, q)], rx.at[k - 1], over_x[k - 1]) for k in (1, 2, 3)])
    quarter[...] = (half[rows(x * q, q), :] + rx[1]) + (rx[0] + rx[2])
    send.run([(quarter.at[rows(lax.rem(z + k, 4) * s, s)], rz.at[k - 1], over_z[k - 1]) for k in (1, 2, 3)])
    ry[y] = (quarter[rows(z * s, s), :] + rz[1]) + (rz[0] + rz[2])
    for k in (0, 1, 2):
        slot = ry.at[lax.rem(y + k, 4)]
        send.run([(slot, slot, down)])


def gather_rows(send, where, out_ref):
    over_core, over_x, over_z, down = where
    z, x, y, core = place()
    n = out_ref.shape[1]
    h, q, s = n // 2, n // 8, n // 32
    base = core * h + x * q
    part = out_ref.at[:, rows(base + z * s, s)]
    send.run([(part, part, over_z[k - 1]) for k in (1, 2, 3)])
    part = out_ref.at[:, rows(base, q)]
    send.run([(part, part, over_x[k - 1]) for k in (1, 2, 3)])
    part = out_ref.at[:, rows(core * h, h)]
    send.run([(part, part, over_core[0])])


def own_rows(n):
    z, x, y, core = place()
    s = n // 32
    return rows(core * (n // 2) + x * (n // 8) + z * s, s)


def split(x):
    high = x.astype(jnp.bfloat16)
    return high, (x - high.astype(jnp.float32)).astype(jnp.bfloat16)


def dot3(a, b, over):
    dims = ((over[:1], over[1:]), ((), ()))
    dot = lambda l, r: lax.dot_general(l, r, dims, preferred_element_type=jnp.float32)
    return dot(a[0], b[0]) + (dot(a[0], b[1]) + dot(a[1], b[0]))


CHUNK = 256
HALF = CHUNK // 2
PAIRED = 7
EARLY = 2
CROSS = 8 * CHUNK + HALF
SENT = 11 * CHUNK


def phase_kernel(x_ref, grams_ref, la_ref, xa_ref, cross_ref, got_ref, own, acc, half, quarter, rc, rx, rz, ry,
                 half2, quarter2, rc2, rx2, rz2, ry2, load_sem, go_sem, come_sem, send_sem, recv_sem):
    where = neighbours(True)
    send = Sender(send_sem, recv_sem)
    snap = lax.axis_index("snap")
    first, second = snap == 0, snap == 1
    other = (lax.axis_index("dof"), 1 - snap)
    count, n = x_ref.shape

    def stream(c, base, size):
        start = c * CHUNK if isinstance(c, int) else pl.multiple_of(c * CHUNK, CHUNK)
        return pltpu.make_async_remote_copy(
            src_ref=x_ref.at[pl.ds(base + start, size)], dst_ref=got_ref.at[pl.ds(start, size)],
            send_sem=go_sem.at[c], recv_sem=come_sem.at[c], device_id=other, device_id_type=MESH)

    def rest():
        start = CROSS
        return pltpu.make_async_remote_copy(
            src_ref=x_ref.at[pl.ds(start, SENT - CROSS)], dst_ref=got_ref.at[pl.ds(start, SENT - CROSS)],
            send_sem=go_sem.at[9], recv_sem=come_sem.at[9], device_id=other, device_id_type=MESH)

    @pl.when(first)
    def _():
        for c in range(8):
            stream(c, 0, CHUNK).start()
        stream(8, 0, HALF).start()
        rest().start()

    @pl.when(second)
    def _():
        for c in range(EARLY):
            stream(c, CROSS, CHUNK).start()

    loads = count // CHUNK

    def load(c):
        at = pl.ds(pl.multiple_of(c * CHUNK, CHUNK), CHUNK)
        return pltpu.make_async_copy(x_ref.at[at], own.at[at], load_sem.at[c])

    def load_one(c, _):
        load(c).start()
        return 0

    lax.fori_loop(0, loads, load_one, 0)
    acc[...] = jnp.zeros_like(acc)

    def gram_one(c, _):
        load(c).wait()
        high, low = split(own[pl.ds(pl.multiple_of(c * CHUNK, CHUNK), CHUNK), :])
        acc[...] += dot_tn(high, high * jnp.bfloat16(0.5)) + dot_tn(high, low)
        return 0

    lax.fori_loop(0, loads, gram_one, 0)
    acc[...] = acc[...] + acc[...].T

    scatter_sum(send, where, acc, half, quarter, rc, rx, rz, ry)
    mine = own_rows(n)
    grams_ref[0, mine, :] = ry[0] + ry[2]
    grams_ref[1, mine, :] = ry[1] + ry[3]

    @pl.when(second)
    def _():
        for c in range(EARLY, PAIRED):
            stream(c, CROSS, CHUNK).start()
        stream(PAIRED, CROSS, HALF).start()

    gather_rows(send, where, grams_ref)
    acc[...] = grams_ref[0]
    factor_into(acc, la_ref, xa_ref, n)

    acc[...] = jnp.zeros_like(acc)

    def add(start, size, own_start):
        got = got_ref[pl.ds(start, size), :]
        mine = own[pl.ds(own_start, size), :]
        left = split(jnp.where(second, mine, got))
        right = split(jnp.where(second, got, mine))
        acc[...] += dot3(left, right, (0, 0))

    def cross_one(c, _):
        stream(c, 0, CHUNK).wait_recv()
        start = pl.multiple_of(c * CHUNK, CHUNK)
        add(start, CHUNK, pl.multiple_of(start + (1 - snap) * CROSS, HALF))
        return 0

    lax.fori_loop(0, PAIRED, cross_one, 0)

    @pl.when(first)
    def _():
        stream(PAIRED, 0, HALF).wait_recv()
        add(PAIRED * CHUNK, HALF, PAIRED * CHUNK + CROSS)

    @pl.when(second)
    def _():
        stream(PAIRED, 0, CHUNK).wait_recv()
        add(PAIRED * CHUNK, CHUNK, PAIRED * CHUNK)
        stream(8, 0, HALF).wait_recv()
        add(8 * CHUNK, HALF, 8 * CHUNK)

    scatter_sum(send, where, acc, half2, quarter2, rc2, rx2, rz2, ry2)
    cross_ref[0, mine, :] = (ry2[0] + ry2[2]) + (ry2[1] + ry2[3])
    gather_rows(send, where, cross_ref)

    @pl.when(first)
    def _():
        for c in range(8):
            stream(c, 0, CHUNK).wait_send()
        stream(8, 0, HALF).wait_send()
        rest().wait_send()

    @pl.when(second)
    def _():
        for c in range(PAIRED):
            stream(c, CROSS, CHUNK).wait_send()
        stream(PAIRED, CROSS, HALF).wait_send()
        rest().wait_recv()


def dot_tn(a, b):
    return lax.dot_general(a, b, (((0,), (0,)), ((), ())), preferred_element_type=jnp.float32)


def phase(snapshots):
    count, n = snapshots.shape
    f32 = jnp.float32
    shape = lambda *s: jax.ShapeDtypeStruct(s, f32)
    parts = [
        pltpu.VMEM((n // 2, n), f32),
        pltpu.VMEM((n // 8, n), f32),
        pltpu.VMEM((n // 2, n), f32),
        pltpu.VMEM((3, n // 8, n), f32),
        pltpu.VMEM((3, n // 32, n), f32),
        pltpu.VMEM((4, n // 32, n), f32),
    ]
    dma = pltpu.SemaphoreType.DMA
    return pl.pallas_call(
        phase_kernel,
        out_shape=(shape(2, n, n), shape(n, n), shape(n, n), shape(1, n, n), shape(SENT, n)),
        in_specs=[pl.BlockSpec(memory_space=pl.ANY)],
        out_specs=(VMEM,) * 5,
        scratch_shapes=[pltpu.VMEM((count, n), f32), pltpu.VMEM((n, n), f32)] + parts + parts
        + [dma((count // CHUNK,)), dma((10,)), dma((10,)), dma((34,)), dma((34,))],
        compiler_params=pltpu.CompilerParams(
            collective_id=0, has_side_effects=True, vmem_limit_bytes=56 << 20),
        cost_estimate=pl.CostEstimate(flops=130 << 30, bytes_accessed=400 << 20, transcendentals=0),
    )(snapshots)


TALL = 256


def basis_kernel(scale, who_ref, own_ref, a_ref, xa_ref, xb_ref, xba_ref, *others):
    out_ref, high, low, high2, low2 = others[-5:]
    second = who_ref[0] == 1

    @pl.when(pl.program_id(0) == 0)
    def _():
        high[...], low[...] = split(jnp.where(second, xb_ref[...], xa_ref[...]) * scale)
        high2[...], low2[...] = split(xba_ref[...] * scale)

    out_ref[...] = dot3(split(own_ref[...]), (high[...], low[...]), (1, 1))

    @pl.when(second)
    def _():
        out_ref[...] += dot3(split(a_ref[...]), (high2[...], low2[...]), (1, 1))


def basis_rows(scale, first_row, snap, own, a, xa, xb, xba, so_far):
    count, n = own.shape
    steps, offset = a.shape[0] // TALL, first_row // TALL
    whole = pl.BlockSpec((n, n), lambda i, who: (0, 0))
    placed = pl.BlockSpec((TALL, n), lambda i, who: (i + offset, 0))
    extra = [] if so_far is None else [so_far]
    return pl.pallas_call(
        functools.partial(basis_kernel, scale),
        out_shape=jax.ShapeDtypeStruct((count, n), jnp.float32),
        grid_spec=pltpu.PrefetchScalarGridSpec(
            num_scalar_prefetch=1,
            grid=(steps,),
            in_specs=[placed, pl.BlockSpec((TALL, n), lambda i, who: (who[0] * i, 0)), whole, whole, whole]
            + [pl.BlockSpec(memory_space=pl.ANY)] * len(extra),
            out_specs=placed,
            scratch_shapes=[pltpu.VMEM((n, n), jnp.bfloat16)] * 4,
        ),
        input_output_aliases={6: 0} if extra else {},
        compiler_params=pltpu.CompilerParams(vmem_limit_bytes=60 << 20),
        cost_estimate=pl.CostEstimate(flops=6 << 30, bytes_accessed=12 << 20, transcendentals=0),
    )(snap, own, a, xa, xb, xba, *extra)


def on_device(snapshots):
    count, n = snapshots.shape
    snap = lax.axis_index("snap")
    first = snap == 0
    who = snap.astype(jnp.int32).reshape(1)
    root_rows = float(count * lax.axis_size("dof")) ** 0.5
    tie = lambda *values: lax.optimization_barrier(values)

    grams, la, xa, cross, a1 = phase(snapshots)
    late, cross = tie(snapshots, cross)
    a2 = lax.ppermute(late[SENT:], "snap", [(0, 1)])
    lba, xba, lb, xb = factor_second(grams, cross, xa)
    top = jnp.where(first, la, lba).T
    bottom = jnp.where(first, 0.0, lb).T
    factor = jnp.concatenate([top, bottom]) / root_rows
    basis = basis_rows(root_rows, 0, who, snapshots, a1, xa, xb, xba, None)
    a2, basis, factor = tie(a2, basis, factor)
    basis = basis_rows(root_rows, SENT, who, snapshots, a2, xa, xb, xba, basis)
    return (basis, factor)


def solution(mesh):
    in_specs = (P("dof", "snap"),)
    out_specs = (P("dof", "snap"), P(None, "snap"))
    return jax.shard_map(
        on_device, mesh=mesh, in_specs=in_specs, out_specs=out_specs, check_vma=False
    )
```

```python
import functools

import jax
import jax.numpy as jnp
from jax import lax
from jax.experimental import pallas as pl
from jax.experimental.pallas import tpu as pltpu
from jax.sharding import PartitionSpec as P

MESH = pl.DeviceIdType.MESH
HI = lax.Precision.HIGHEST
T = 128

def dot_nt(a, b):
    return lax.dot_general(a, b, (((1,), (1,)), ((), ())), preferred_element_type=jnp.float32, precision=HI)

def dot_nn(a, b):
    return lax.dot_general(a, b, (((1,), (0,)), ((), ())), preferred_element_type=jnp.float32, precision=HI)

def eliminate(block):
    sub = lax.broadcasted_iota(jnp.int32, (8, T), 0)
    lane = lax.broadcasted_iota(jnp.int32, (8, T), 1)
    rows = [block[8 * i:8 * i + 8, :] for i in range(T // 8)]
    upper, lower, pivots = [], [], []
    for b in range(T // 8):
        first = 8 * b
        in_block = (lane >= first) & (lane < first + 8)
        head = rows[b]
        cols = [jnp.broadcast_to(head[:, first + k:first + k + 1], (8, T)) for k in range(8)]
        t = {}
        for k in range(8):
            for j in range(k + 1):
                t[j, k] = jnp.broadcast_to(cols[k][j:j + 1, :], (8, T))
        recip = []
        for j in range(8):
            r = 1.0 / t[j, j]
            recip.append(r)
            for k in range(j + 1, 8):
                s = t[j, k] * r
                for l in range(k, 8):
                    t[k, l] = t[k, l] - s * t[j, l]
        pivot = t[0, 0]
        for j in range(1, 8):
            pivot = jnp.where(sub == j, t[j, j], pivot)
        pivots.append(pivot)

        def multipliers(cs, below):
            cs = list(cs)
            out = []
            for j in range(8):
                m = cs[j] * recip[j]
                if not below:
                    m = jnp.where(sub > j, m, 0.0)
                out.append(m)
                for k in range(j + 1, 8):
                    cs[k] = cs[k] - m * t[j, k]
            return out

        v = jnp.where(in_block, jnp.where(lane == sub + first, 1.0, 0.0), head)
        m = multipliers(cols, False)
        own = head
        for j in range(8):
            v = v - m[j] * jnp.broadcast_to(v[j:j + 1, :], (8, T))
            own = own - m[j] * jnp.broadcast_to(own[j:j + 1, :], (8, T))
        vb = [jnp.broadcast_to(v[j:j + 1, :], (8, T)) for j in range(8)]
        upper.append(jnp.where(lane >= sub + first, own, 0.0))
        lower.append(jnp.where(lane <= sub + first, v, 0.0))
        for i in range(b + 1, T // 8):
            cs = [jnp.broadcast_to(rows[i][:, first + k:first + k + 1], (8, T)) for k in range(8)]
            m = multipliers(cs, True)
            w = jnp.where(in_block, 0.0, rows[i])
            for j in range(8):
                w = w - m[j] * vb[j]
            rows[i] = w
    cat = lambda x: jnp.concatenate(x, axis=0)
    return cat(lower), cat(upper), cat(pivots)

def factor_into(a_ref, l_ref, x_ref, n, lt_ref=None):
    steps = n // T
    def step(p, _):
        at = pl.ds(pl.multiple_of(p * T, T), T)
        low, up, piv = eliminate(a_ref[at, at])
        scale = lax.rsqrt(piv)
        xd = low * scale
        ld = up * scale
        x_ref[at, at] = xd
        l_ref[at, at] = ld.T
        for k in range(steps):
            @pl.when(p == k)
            def _():
                o = k * T
                e = o + T
                if k > 0:
                    part = dot_nn(l_ref[o:e, 0:o], x_ref[0:o, 0:o])
                    x_ref[o:e, 0:o] = -dot_nn(xd, part)
                if e < n:
                    x_ref[o:e, e:n] = jnp.zeros((T, n - e), jnp.float32)
                    l_ref[o:e, e:n] = jnp.zeros((T, n - e), jnp.float32)
                    l21 = dot_nt(a_ref[e:n, o:e], xd)
                    l_ref[e:n, o:e] = l21
                    a_ref[e:n, e:n] = a_ref[e:n, e:n] - dot_nt(l21, l21)
        return 0
    lax.fori_loop(0, steps, step, 0)


VMEM = pl.BlockSpec(memory_space=pltpu.VMEM)


def place():
    dof, snap = lax.axis_index("dof"), lax.axis_index("snap")
    core, y_hi = lax.rem(dof, 2), lax.rem(dof // 2, 2)
    return dof // 16, lax.rem(dof // 4, 4), y_hi * 2 + snap, core


def device(z, x, y, core):
    return (z * 16 + x * 4 + (y // 2) * 2 + core, lax.rem(y, 2))


def neighbours(with_y):
    z, x, y, core = place()
    over_core = [device(z, x, y, 1 - core)]
    over_x = [device(z, lax.rem(x + k, 4), y, core) for k in (1, 2, 3)]
    over_z = [device(lax.rem(z + k, 4), x, y, core) for k in (1, 2, 3)]
    down = device(z, x, lax.rem(y + 3, 4), core)
    greet = over_core + over_x + over_z
    if with_y:
        greet = greet + [down, device(z, x, lax.rem(y + 1, 4), core)]
    barrier = pltpu.get_barrier_semaphore()
    for partner in greet:
        pl.semaphore_signal(barrier, inc=1, device_id=partner, device_id_type=MESH)
    pl.semaphore_wait(barrier, len(greet))
    return over_core, over_x, over_z, down


class Sender:
    def __init__(self, send_sem, recv_sem):
        self.sems, self.used = (send_sem, recv_sem), 0

    def start(self, src, dst, to):
        send_sem, recv_sem = (s.at[self.used] for s in self.sems)
        self.used += 1
        copy = pltpu.make_async_remote_copy(
            src_ref=src, dst_ref=dst, send_sem=send_sem, recv_sem=recv_sem, device_id=to, device_id_type=MESH)
        copy.start()
        return copy

    def run(self, triples):
        for copy in [self.start(*t) for t in triples]:
            copy.wait()


def rows(start, size):
    return pl.ds(pl.multiple_of(start, size), size)


def scatter_sum(send, where, p_ref, half, quarter, rc, r1, r2, ry):
    over_core, over_x, over_z, down = where
    z, x, y, core = place()
    n = p_ref.shape[0]
    h, q, s, w = n // 2, n // 8, n // 32, n // 2
    left, right = pl.ds(0, w), pl.ds(w, w)
    send.run([(p_ref.at[rows((1 - core) * h, h)], rc, over_core[0])])
    half[...] = p_ref[rows(core * h, h), :] + rc[...]
    jobs = []
    for k in (2, 1, 3):
        jobs.append((half.at[rows(lax.rem(x + k, 4) * q, q), left], r1.at[0, k - 1], over_x[k - 1]))
        jobs.append((half.at[rows(lax.rem(z + k, 4) * q, q), right], r1.at[1, k - 1], over_z[k - 1]))
    send.run(jobs)
    quarter[0] = (half[rows(x * q, q), left] + r1[0, 1]) + (r1[0, 0] + r1[0, 2])
    quarter[1] = (half[rows(z * q, q), right] + r1[1, 1]) + (r1[1, 0] + r1[1, 2])
    jobs = []
    for k in (2, 1, 3):
        jobs.append((quarter.at[0, rows(lax.rem(z + k, 4) * s, s)], r2.at[0, k - 1], over_z[k - 1]))
        jobs.append((quarter.at[1, rows(lax.rem(x + k, 4) * s, s)], r2.at[1, k - 1], over_x[k - 1]))
    send.run(jobs)
    ry[y, 0] = (quarter[0, rows(z * s, s), :] + r2[0, 1]) + (r2[0, 0] + r2[0, 2])
    ry[y, 1] = (quarter[1, rows(x * s, s), :] + r2[1, 1]) + (r2[1, 0] + r2[1, 2])
    for k in (0, 1, 2):
        slot = ry.at[lax.rem(y + k, 4)]
        send.run([(slot, slot, down)])


def put_piece(out_ref, block, ry, slots):
    z, x, y, core = place()
    n = out_ref.shape[1]
    h, q, s, w = n // 2, n // 8, n // 32, n // 2
    at = (core * h + x * q + z * s, core * h + z * q + x * s)
    for side in (0, 1):
        total = ry[slots[0], side] + ry[slots[1], side]
        for i in range(2, len(slots), 2):
            total = total + (ry[slots[i], side] + ry[slots[i + 1], side])
        out_ref[block, rows(at[side], s), pl.ds(side * w, w)] = total


def gather_rows(send, where, out_ref):
    over_core, over_x, over_z, down = where
    z, x, y, core = place()
    n = out_ref.shape[1]
    h, q, s, w = n // 2, n // 8, n // 32, n // 2
    left, right = pl.ds(0, w), pl.ds(w, w)
    lpart = out_ref.at[:, rows(core * h + x * q + z * s, s), left]
    rpart = out_ref.at[:, rows(core * h + z * q + x * s, s), right]
    jobs = []
    for k in (2, 1, 3):
        jobs += [(lpart, lpart, over_z[k - 1]), (rpart, rpart, over_x[k - 1])]
    send.run(jobs)
    lpart = out_ref.at[:, rows(core * h + x * q, q), left]
    rpart = out_ref.at[:, rows(core * h + z * q, q), right]
    jobs = []
    for k in (2, 1, 3):
        jobs += [(lpart, lpart, over_x[k - 1]), (rpart, rpart, over_z[k - 1])]
    send.run(jobs)
    part = out_ref.at[:, rows(core * h, h)]
    send.run([(part, part, over_core[0])])


def split(x):
    high = x.astype(jnp.bfloat16)
    return high, (x - high.astype(jnp.float32)).astype(jnp.bfloat16)


def dot3(a, b, over):
    dims = ((over[:1], over[1:]), ((), ()))
    dot = lambda l, r: lax.dot_general(l, r, dims, preferred_element_type=jnp.float32)
    return dot(a[0], b[0]) + (dot(a[0], b[1]) + dot(a[1], b[0]))


CHUNK = 256
EARLY = 2


def dot_tn(a, b):
    return lax.dot_general(a, b, (((0,), (0,)), ((), ())), preferred_element_type=jnp.float32)


def thrice(x):
    high, low = split(x)
    return [high, high, low]


def weights(x):
    high, low = split(x)
    return jnp.concatenate([high, low, high], axis=1)


def whole_kernel(root, x_ref, own, factor_ref, got, grams, la, xa, cross, lba, lb, xb, xba, acc, w,
                 half, quarter, rc, r1, r2, ry, half_b, quarter_b, rc_b, r1_b, r2_b, ry_b,
                 load_sem, go_sem, come_sem, send_sem, recv_sem):
    where = neighbours(True)
    send = Sender(send_sem, recv_sem)
    snap = lax.axis_index("snap")
    first, second = snap == 0, snap == 1
    other = (lax.axis_index("dof"), 1 - snap)
    count, n = x_ref.shape
    chunks = count // CHUNK
    paired = chunks // 2
    chunk = lambda c: pl.ds(pl.multiple_of(c * CHUNK, CHUNK), CHUNK)

    def stream(c, ahead):
        return pltpu.make_async_remote_copy(
            src_ref=x_ref.at[chunk(c + ahead)], dst_ref=got.at[chunk(c)],
            send_sem=go_sem.at[c], recv_sem=come_sem.at[c], device_id=other, device_id_type=MESH)

    def loop(begin, end, body):
        def step(c, carry):
            body(c)
            return carry

        lax.fori_loop(begin, end, step, 0)

    @pl.when(first)
    def _():
        loop(0, chunks, lambda c: stream(c, 0).start())

    @pl.when(second)
    def _():
        loop(0, EARLY, lambda c: stream(c, paired).start())

    load = lambda c: pltpu.make_async_copy(x_ref.at[chunk(c)], own.at[chunk(c)], load_sem.at[c])
    loop(0, chunks, lambda c: load(c).start())
    acc[...] = jnp.zeros_like(acc)

    def gram_one(c):
        load(c).wait()
        high, low = split(own[chunk(c), :])
        acc[...] += dot_tn(high, high * jnp.bfloat16(0.5)) + dot_tn(high, low)

    loop(0, chunks, gram_one)
    acc[...] = acc[...] + acc[...].T

    scatter_sum(send, where, acc, half, quarter, rc, r1, r2, ry)
    put_piece(grams, 0, ry, (0, 2))
    put_piece(grams, 1, ry, (1, 3))

    @pl.when(second)
    def _():
        loop(EARLY, paired, lambda c: stream(c, paired).start())

    gather_rows(send, where, grams)
    acc[...] = grams[0]
    factor_into(acc, la, xa, n)

    def basis_one(c, values, width):
        own[chunk(c), :] = lax.dot_general(
            jnp.concatenate(values, axis=1), w[:, :width], (((1,), (1,)), ((), ())),
            preferred_element_type=jnp.float32)

    @pl.when(first)
    def _():
        w[:, :3 * n] = weights(xa[...] * root)
        factor_ref[:n, :] = la[...].T / root
        factor_ref[n:, :] = jnp.zeros((n, n), jnp.float32)

    acc[...] = jnp.zeros_like(acc)

    def cross_one(c):
        stream(c, 0).wait_recv()
        there = got[chunk(c), :]
        here = own[chunk(c + (1 - snap) * paired), :]
        left = split(jnp.where(second, here, there))
        right = split(jnp.where(second, there, here))
        acc[...] += dot3(left, right, (0, 0))

    loop(0, paired, cross_one)
    scatter_sum(send, where, acc, half_b, quarter_b, rc_b, r1_b, r2_b, ry_b)
    put_piece(cross, 0, ry_b, (0, 2, 1, 3))
    gather_rows(send, where, cross)

    @pl.when(second)
    def _():
        lba[...] = dot_nt(cross[0], xa[...])
        acc[...] = grams[1] - dot_nt(lba[...], lba[...])
        factor_into(acc, lb, xb, n)
        xba[...] = -dot_nn(xb[...], dot_nn(lba[...], xa[...]))
        w[:, :3 * n] = weights(xb[...] * root)
        w[:, 3 * n:] = weights(xba[...] * root)
        factor_ref[:n, :] = lba[...].T / root
        factor_ref[n:, :] = lb[...].T / root

        def one(c):
            @pl.when(c >= paired)
            def _():
                stream(c, 0).wait_recv()

            basis_one(c, thrice(own[chunk(c), :]) + thrice(got[chunk(c), :]), 6 * n)

        loop(0, chunks, one)
        loop(0, paired, lambda c: stream(c, paired).wait_send())

    @pl.when(first)
    def _():
        loop(0, chunks, lambda c: basis_one(c, thrice(own[chunk(c), :]), 3 * n))
        loop(0, chunks, lambda c: stream(c, 0).wait_send())


def whole(snapshots, root):
    count, n = snapshots.shape
    chunks = count // CHUNK
    f32 = jnp.float32
    sums = [
        pltpu.VMEM((n // 2, n), f32),
        pltpu.VMEM((2, n // 8, n // 2), f32),
        pltpu.VMEM((n // 2, n), f32),
        pltpu.VMEM((2, 3, n // 8, n // 2), f32),
        pltpu.VMEM((2, 3, n // 32, n // 2), f32),
        pltpu.VMEM((4, 2, n // 32, n // 2), f32),
    ]
    square = pltpu.VMEM((n, n), f32)
    dma = pltpu.SemaphoreType.DMA
    return pl.pallas_call(
        functools.partial(whole_kernel, root),
        out_shape=(jax.ShapeDtypeStruct((count, n), f32), jax.ShapeDtypeStruct((2 * n, n), f32)),
        in_specs=[pl.BlockSpec(memory_space=pl.ANY)],
        out_specs=(VMEM, VMEM),
        scratch_shapes=[pltpu.VMEM((count, n), f32)]
        + [pltpu.VMEM((2, n, n), f32), square, square, pltpu.VMEM((1, n, n), f32)] + [square] * 5
        + [pltpu.VMEM((n, 6 * n), jnp.bfloat16)] + sums + sums
        + [dma((chunks,)), dma((chunks,)), dma((chunks,)), dma((58,)), dma((58,))],
        compiler_params=pltpu.CompilerParams(
            collective_id=0, has_side_effects=True, vmem_limit_bytes=40 << 20),
        cost_estimate=pl.CostEstimate(flops=130 << 30, bytes_accessed=400 << 20, transcendentals=0),
    )(snapshots)


def on_device(snapshots):
    root_rows = float(snapshots.shape[0] * lax.axis_size("dof")) ** 0.5
    return tuple(whole(snapshots, root_rows))


def solution(mesh):
    in_specs = (P("dof", "snap"),)
    out_specs = (P("dof", "snap"), P(None, "snap"))
    return jax.shard_map(
        on_device, mesh=mesh, in_specs=in_specs, out_specs=out_specs, check_vma=False
    )
```

```python
import functools

import jax
import jax.numpy as jnp
from jax import lax
from jax.experimental import pallas as pl
from jax.experimental.pallas import tpu as pltpu
from jax.sharding import PartitionSpec as P

MESH = pl.DeviceIdType.MESH
HI = lax.Precision.HIGHEST
T = 128

def dot_nt(a, b):
    return lax.dot_general(a, b, (((1,), (1,)), ((), ())), preferred_element_type=jnp.float32, precision=HI)

def dot_nn(a, b):
    return lax.dot_general(a, b, (((1,), (0,)), ((), ())), preferred_element_type=jnp.float32, precision=HI)

def eliminate(block):
    sub = lax.broadcasted_iota(jnp.int32, (8, T), 0)
    lane = lax.broadcasted_iota(jnp.int32, (8, T), 1)
    rows = [block[8 * i:8 * i + 8, :] for i in range(T // 8)]
    upper, lower, pivots = [], [], []
    for b in range(T // 8):
        first = 8 * b
        in_block = (lane >= first) & (lane < first + 8)
        head = rows[b]
        cols = [jnp.broadcast_to(head[:, first + k:first + k + 1], (8, T)) for k in range(8)]
        t = {}
        for k in range(8):
            for j in range(k + 1):
                t[j, k] = jnp.broadcast_to(cols[k][j:j + 1, :], (8, T))
        recip = []
        for j in range(8):
            r = 1.0 / t[j, j]
            recip.append(r)
            for k in range(j + 1, 8):
                s = t[j, k] * r
                for l in range(k, 8):
                    t[k, l] = t[k, l] - s * t[j, l]
        pivot = t[0, 0]
        for j in range(1, 8):
            pivot = jnp.where(sub == j, t[j, j], pivot)
        pivots.append(pivot)

        def multipliers(cs, below):
            cs = list(cs)
            out = []
            for j in range(8):
                m = cs[j] * recip[j]
                if not below:
                    m = jnp.where(sub > j, m, 0.0)
                out.append(m)
                for k in range(j + 1, 8):
                    cs[k] = cs[k] - m * t[j, k]
            return out

        v = jnp.where(in_block, jnp.where(lane == sub + first, 1.0, 0.0), head)
        m = multipliers(cols, False)
        own = head
        for j in range(8):
            v = v - m[j] * jnp.broadcast_to(v[j:j + 1, :], (8, T))
            own = own - m[j] * jnp.broadcast_to(own[j:j + 1, :], (8, T))
        vb = [jnp.broadcast_to(v[j:j + 1, :], (8, T)) for j in range(8)]
        upper.append(jnp.where(lane >= sub + first, own, 0.0))
        lower.append(jnp.where(lane <= sub + first, v, 0.0))
        for i in range(b + 1, T // 8):
            cs = [jnp.broadcast_to(rows[i][:, first + k:first + k + 1], (8, T)) for k in range(8)]
            m = multipliers(cs, True)
            w = jnp.where(in_block, 0.0, rows[i])
            for j in range(8):
                w = w - m[j] * vb[j]
            rows[i] = w
    cat = lambda x: jnp.concatenate(x, axis=0)
    return cat(lower), cat(upper), cat(pivots)

def factor_into(a_ref, l_ref, x_ref, n, lt_ref=None):
    steps = n // T
    def step(p, _):
        at = pl.ds(pl.multiple_of(p * T, T), T)
        low, up, piv = eliminate(a_ref[at, at])
        scale = lax.rsqrt(piv)
        xd = low * scale
        ld = up * scale
        x_ref[at, at] = xd
        l_ref[at, at] = ld.T
        for k in range(steps):
            @pl.when(p == k)
            def _():
                o = k * T
                e = o + T
                if k > 0:
                    part = dot_nn(l_ref[o:e, 0:o], x_ref[0:o, 0:o])
                    x_ref[o:e, 0:o] = -dot_nn(xd, part)
                if e < n:
                    x_ref[o:e, e:n] = jnp.zeros((T, n - e), jnp.float32)
                    l_ref[o:e, e:n] = jnp.zeros((T, n - e), jnp.float32)
                    l21 = dot_nt(a_ref[e:n, o:e], xd)
                    l_ref[e:n, o:e] = l21
                    a_ref[e:n, e:n] = a_ref[e:n, e:n] - dot_nt(l21, l21)
        return 0
    lax.fori_loop(0, steps, step, 0)


VMEM = pl.BlockSpec(memory_space=pltpu.VMEM)


def place():
    dof, snap = lax.axis_index("dof"), lax.axis_index("snap")
    core, y_hi = lax.rem(dof, 2), lax.rem(dof // 2, 2)
    return dof // 16, lax.rem(dof // 4, 4), y_hi * 2 + snap, core


def device(z, x, y, core):
    return (z * 16 + x * 4 + (y // 2) * 2 + core, lax.rem(y, 2))


def neighbours(with_y):
    z, x, y, core = place()
    over_core = [device(z, x, y, 1 - core)]
    over_x = [device(z, lax.rem(x + k, 4), y, core) for k in (1, 2, 3)]
    over_z = [device(lax.rem(z + k, 4), x, y, core) for k in (1, 2, 3)]
    down = device(z, x, lax.rem(y + 3, 4), core)
    greet = over_core + over_x + over_z
    if with_y:
        greet = greet + [down, device(z, x, lax.rem(y + 1, 4), core)]
    barrier = pltpu.get_barrier_semaphore()
    for partner in greet:
        pl.semaphore_signal(barrier, inc=1, device_id=partner, device_id_type=MESH)
    pl.semaphore_wait(barrier, len(greet))
    return over_core, over_x, over_z, down


class Sender:
    def __init__(self, send_sem, recv_sem):
        self.sems, self.used = (send_sem, recv_sem), 0

    def start(self, src, dst, to):
        send_sem, recv_sem = (s.at[self.used] for s in self.sems)
        self.used += 1
        copy = pltpu.make_async_remote_copy(
            src_ref=src, dst_ref=dst, send_sem=send_sem, recv_sem=recv_sem, device_id=to, device_id_type=MESH)
        copy.start()
        return copy

    def run(self, triples):
        for copy in [self.start(*t) for t in triples]:
            copy.wait()


def rows(start, size):
    return pl.ds(pl.multiple_of(start, size), size)


def scatter_sum(send, where, p_ref, half, quarter, rc, r1, r2, ry):
    over_core, over_x, over_z, down = where
    z, x, y, core = place()
    n = p_ref.shape[0]
    h, q, s, w = n // 2, n // 8, n // 32, n // 2
    left, right = pl.ds(0, w), pl.ds(w, w)
    send.run([(p_ref.at[rows((1 - core) * h, h)], rc, over_core[0])])
    half[...] = p_ref[rows(core * h, h), :] + rc[...]
    jobs = []
    for k in (2, 1, 3):
        jobs.append((half.at[rows(lax.rem(x + k, 4) * q, q), left], r1.at[0, k - 1], over_x[k - 1]))
        jobs.append((half.at[rows(lax.rem(z + k, 4) * q, q), right], r1.at[1, k - 1], over_z[k - 1]))
    send.run(jobs)
    quarter[0] = (half[rows(x * q, q), left] + r1[0, 1]) + (r1[0, 0] + r1[0, 2])
    quarter[1] = (half[rows(z * q, q), right] + r1[1, 1]) + (r1[1, 0] + r1[1, 2])
    jobs = []
    for k in (2, 1, 3):
        jobs.append((quarter.at[0, rows(lax.rem(z + k, 4) * s, s)], r2.at[0, k - 1], over_z[k - 1]))
        jobs.append((quarter.at[1, rows(lax.rem(x + k, 4) * s, s)], r2.at[1, k - 1], over_x[k - 1]))
    send.run(jobs)
    ry[y, 0] = (quarter[0, rows(z * s, s), :] + r2[0, 1]) + (r2[0, 0] + r2[0, 2])
    ry[y, 1] = (quarter[1, rows(x * s, s), :] + r2[1, 1]) + (r2[1, 0] + r2[1, 2])
    for k in (0, 1, 2):
        slot = ry.at[lax.rem(y + k, 4)]
        send.run([(slot, slot, down)])


def put_piece(out_ref, block, ry, slots):
    z, x, y, core = place()
    n = out_ref.shape[1]
    h, q, s, w = n // 2, n // 8, n // 32, n // 2
    at = (core * h + x * q + z * s, core * h + z * q + x * s)
    for side in (0, 1):
        total = ry[slots[0], side] + ry[slots[1], side]
        for i in range(2, len(slots), 2):
            total = total + (ry[slots[i], side] + ry[slots[i + 1], side])
        out_ref[block, rows(at[side], s), pl.ds(side * w, w)] = total


def gather_rows(send, where, out_ref):
    over_core, over_x, over_z, down = where
    z, x, y, core = place()
    n = out_ref.shape[1]
    h, q, s, w = n // 2, n // 8, n // 32, n // 2
    left, right = pl.ds(0, w), pl.ds(w, w)
    lpart = out_ref.at[:, rows(core * h + x * q + z * s, s), left]
    rpart = out_ref.at[:, rows(core * h + z * q + x * s, s), right]
    jobs = []
    for k in (2, 1, 3):
        jobs += [(lpart, lpart, over_z[k - 1]), (rpart, rpart, over_x[k - 1])]
    send.run(jobs)
    lpart = out_ref.at[:, rows(core * h + x * q, q), left]
    rpart = out_ref.at[:, rows(core * h + z * q, q), right]
    jobs = []
    for k in (2, 1, 3):
        jobs += [(lpart, lpart, over_x[k - 1]), (rpart, rpart, over_z[k - 1])]
    send.run(jobs)
    part = out_ref.at[:, rows(core * h, h)]
    send.run([(part, part, over_core[0])])


def split(x):
    high = x.astype(jnp.bfloat16)
    return high, (x - high.astype(jnp.float32)).astype(jnp.bfloat16)


def dot3(a, b, over):
    dims = ((over[:1], over[1:]), ((), ()))
    dot = lambda l, r: lax.dot_general(l, r, dims, preferred_element_type=jnp.float32)
    return dot(a[0], b[0]) + (dot(a[0], b[1]) + dot(a[1], b[0]))


CHUNK = 256
EARLY = 2
ROUND = 2


def dot_tn(a, b):
    return lax.dot_general(a, b, (((0,), (0,)), ((), ())), preferred_element_type=jnp.float32)


def thrice(x):
    high, low = split(x)
    return [high, high, low]


def weights(x):
    high, low = split(x)
    return jnp.concatenate([high, low, high], axis=1)


def whole_kernel(root, x_ref, own, factor_ref, got, relay, grams, la, xa, cross, lba, lb, xb, xba, acc, w,
                 half, quarter, rc, r1, r2, ry, half_b, quarter_b, rc_b, r1_b, r2_b, ry_b,
                 load_sem, go_sem, come_sem, hop_go_sem, hop_come_sem, send_sem, recv_sem):
    send = Sender(send_sem, recv_sem)
    snap = lax.axis_index("snap")
    first, second = snap == 0, snap == 1
    other = (lax.axis_index("dof"), 1 - snap)
    count, n = x_ref.shape
    chunks = count // CHUNK
    paired = chunks // 2
    direct = chunks - ROUND
    chunk = lambda c: pl.ds(pl.multiple_of(c * CHUNK, CHUNK), CHUNK)
    pair = lambda c: pl.ds(pl.multiple_of(c * 2 * CHUNK, 2 * CHUNK), 2 * CHUNK)

    def stream(c, ahead):
        return pltpu.make_async_remote_copy(
            src_ref=x_ref.at[chunk(c + ahead)], dst_ref=got.at[chunk(c)],
            send_sem=go_sem.at[c], recv_sem=come_sem.at[c], device_id=other, device_id_type=MESH)

    def loop(begin, end, body):
        def step(c, carry):
            body(c)
            return carry

        lax.fori_loop(begin, end, step, 0)

    load = lambda c: pltpu.make_async_copy(x_ref.at[chunk(c)], own.at[chunk(c)], load_sem.at[c])
    loop(0, chunks, lambda c: load(c).start())
    where = neighbours(True)
    down = where[3]

    def hop(which, i):
        src = (x_ref.at[chunk(direct + i)], relay.at[i], relay.at[i])[which]
        dst = (relay.at[i], relay.at[i], got.at[chunk(direct + i)])[which]
        go = hop_go_sem.at[i if which < 2 else ROUND + i]
        come = hop_come_sem.at[i] if which < 2 else come_sem.at[direct + i]
        return pltpu.make_async_remote_copy(
            src_ref=src, dst_ref=dst, send_sem=go, recv_sem=come, device_id=down, device_id_type=MESH)

    @pl.when(first)
    def _():
        loop(0, direct, lambda c: stream(c, 0).start())

    @pl.when(second)
    def _():
        loop(0, EARLY, lambda c: stream(c, paired).start())

    acc[...] = jnp.zeros_like(acc)

    def gram_one(c):
        load(c).wait()
        high, low = split(own[chunk(c), :])
        acc[...] += dot_tn(high, high * jnp.bfloat16(0.5)) + dot_tn(high, low)

    loop(0, chunks, gram_one)
    acc[...] = acc[...] + acc[...].T

    scatter_sum(send, where, acc, half, quarter, rc, r1, r2, ry)
    put_piece(grams, 0, ry, (0, 2))
    put_piece(grams, 1, ry, (1, 3))

    @pl.when(second)
    def _():
        loop(EARLY, paired, lambda c: stream(c, paired).start())

    @pl.when(first)
    def _():
        for i in range(ROUND):
            hop(0, i).start()

    gather_rows(send, where, grams)
    acc[...] = grams[0]
    factor_into(acc, la, xa, n)

    def basis_one(c, values, width):
        own[pair(c), :] = lax.dot_general(
            jnp.concatenate(values, axis=1), w[:, :width], (((1,), (1,)), ((), ())),
            preferred_element_type=jnp.float32)

    @pl.when(first)
    def _():
        w[:, :3 * n] = weights(xa[...] * root)
        factor_ref[:n, :] = la[...].T / root
        factor_ref[n:, :] = jnp.zeros((n, n), jnp.float32)

    acc[...] = jnp.zeros_like(acc)

    def cross_one(c):
        stream(c, 0).wait_recv()
        there = got[chunk(c), :]
        here = own[chunk(c + (1 - snap) * paired), :]
        left = split(jnp.where(second, here, there))
        right = split(jnp.where(second, there, here))
        acc[...] += dot3(left, right, (0, 0))

    @pl.when(second)
    def _():
        hop(0, 0).wait_recv()
        hop(1, 0).start()

    loop(0, paired, cross_one)
    scatter_sum(send, where, acc, half_b, quarter_b, rc_b, r1_b, r2_b, ry_b)
    put_piece(cross, 0, ry_b, (0, 2, 1, 3))

    @pl.when(second)
    def _():
        for i in range(1, ROUND):
            hop(0, i).wait_recv()
            hop(1, i).start()

    @pl.when(first)
    def _():
        hop(1, 0).wait_recv()
        hop(2, 0).start()

    gather_rows(send, where, cross)

    @pl.when(first)
    def _():
        for i in range(1, ROUND):
            hop(1, i).wait_recv()
            hop(2, i).start()

    @pl.when(second)
    def _():
        lba[...] = dot_nt(cross[0], xa[...])
        acc[...] = grams[1] - dot_nt(lba[...], lba[...])
        factor_into(acc, lb, xb, n)
        xba[...] = -dot_nn(xb[...], dot_nn(lba[...], xa[...]))
        w[:, :3 * n] = weights(xb[...] * root)
        w[:, 3 * n:] = weights(xba[...] * root)
        factor_ref[:n, :] = lba[...].T / root
        factor_ref[n:, :] = lb[...].T / root

        def one(c):
            @pl.when(c >= paired // 2)
            def _():
                stream(2 * c, 0).wait_recv()
                stream(2 * c + 1, 0).wait_recv()

            basis_one(c, thrice(own[pair(c), :]) + thrice(got[pair(c), :]), 6 * n)

        loop(0, paired, one)
        loop(0, paired, lambda c: stream(c, paired).wait_send())
        for i in range(ROUND):
            hop(1, i).wait_send()

    @pl.when(first)
    def _():
        loop(0, paired, lambda c: basis_one(c, thrice(own[pair(c), :]), 3 * n))
        loop(0, direct, lambda c: stream(c, 0).wait_send())
        for i in range(ROUND):
            hop(0, i).wait_send()
            hop(2, i).wait_send()


def whole(snapshots, root):
    count, n = snapshots.shape
    chunks = count // CHUNK
    f32 = jnp.float32
    sums = [
        pltpu.VMEM((n // 2, n), f32),
        pltpu.VMEM((2, n // 8, n // 2), f32),
        pltpu.VMEM((n // 2, n), f32),
        pltpu.VMEM((2, 3, n // 8, n // 2), f32),
        pltpu.VMEM((2, 3, n // 32, n // 2), f32),
        pltpu.VMEM((4, 2, n // 32, n // 2), f32),
    ]
    square = pltpu.VMEM((n, n), f32)
    dma = pltpu.SemaphoreType.DMA
    return pl.pallas_call(
        functools.partial(whole_kernel, root),
        out_shape=(jax.ShapeDtypeStruct((count, n), f32), jax.ShapeDtypeStruct((2 * n, n), f32)),
        in_specs=[pl.BlockSpec(memory_space=pl.ANY)],
        out_specs=(VMEM, VMEM),
        scratch_shapes=[pltpu.VMEM((count, n), f32), pltpu.VMEM((ROUND, CHUNK, n), f32)]
        + [pltpu.VMEM((2, n, n), f32), square, square, pltpu.VMEM((1, n, n), f32)] + [square] * 5
        + [pltpu.VMEM((n, 6 * n), jnp.bfloat16)] + sums + sums
        + [dma((chunks,)), dma((chunks,)), dma((chunks,)), dma((2 * ROUND,)), dma((ROUND,)), dma((58,)), dma((58,))],
        compiler_params=pltpu.CompilerParams(
            collective_id=0, has_side_effects=True, vmem_limit_bytes=40 << 20),
        cost_estimate=pl.CostEstimate(flops=130 << 30, bytes_accessed=400 << 20, transcendentals=0),
    )(snapshots)


def on_device(snapshots):
    root_rows = float(snapshots.shape[0] * lax.axis_size("dof")) ** 0.5
    return tuple(whole(snapshots, root_rows))


def solution(mesh):
    in_specs = (P("dof", "snap"),)
    out_specs = (P("dof", "snap"), P(None, "snap"))
    return jax.shard_map(
        on_device, mesh=mesh, in_specs=in_specs, out_specs=out_specs, check_vma=False
    )
```

```python
import functools

import jax
import jax.numpy as jnp
from jax import lax
from jax.experimental import pallas as pl
from jax.experimental.pallas import tpu as pltpu
from jax.sharding import PartitionSpec as P

MESH = pl.DeviceIdType.MESH
HI = lax.Precision.HIGHEST
T = 128

def dot_nt(a, b):
    return lax.dot_general(a, b, (((1,), (1,)), ((), ())), preferred_element_type=jnp.float32, precision=HI)

def dot_nn(a, b):
    return lax.dot_general(a, b, (((1,), (0,)), ((), ())), preferred_element_type=jnp.float32, precision=HI)

def eliminate(block):
    sub = lax.broadcasted_iota(jnp.int32, (8, T), 0)
    lane = lax.broadcasted_iota(jnp.int32, (8, T), 1)
    rows = [block[8 * i:8 * i + 8, :] for i in range(T // 8)]
    upper, lower, pivots = [], [], []
    for b in range(T // 8):
        first = 8 * b
        in_block = (lane >= first) & (lane < first + 8)
        head = rows[b]
        cols = [jnp.broadcast_to(head[:, first + k:first + k + 1], (8, T)) for k in range(8)]
        t = {}
        for k in range(8):
            for j in range(k + 1):
                t[j, k] = jnp.broadcast_to(cols[k][j:j + 1, :], (8, T))
        recip = []
        for j in range(8):
            r = 1.0 / t[j, j]
            recip.append(r)
            for k in range(j + 1, 8):
                s = t[j, k] * r
                for l in range(k, 8):
                    t[k, l] = t[k, l] - s * t[j, l]
        pivot = t[0, 0]
        for j in range(1, 8):
            pivot = jnp.where(sub == j, t[j, j], pivot)
        pivots.append(pivot)

        def multipliers(cs, below):
            cs = list(cs)
            out = []
            for j in range(8):
                m = cs[j] * recip[j]
                if not below:
                    m = jnp.where(sub > j, m, 0.0)
                out.append(m)
                for k in range(j + 1, 8):
                    cs[k] = cs[k] - m * t[j, k]
            return out

        v = jnp.where(in_block, jnp.where(lane == sub + first, 1.0, 0.0), head)
        m = multipliers(cols, False)
        own = head
        for j in range(8):
            v = v - m[j] * jnp.broadcast_to(v[j:j + 1, :], (8, T))
            own = own - m[j] * jnp.broadcast_to(own[j:j + 1, :], (8, T))
        vb = [jnp.broadcast_to(v[j:j + 1, :], (8, T)) for j in range(8)]
        upper.append(jnp.where(lane >= sub + first, own, 0.0))
        lower.append(jnp.where(lane <= sub + first, v, 0.0))
        for i in range(b + 1, T // 8):
            cs = [jnp.broadcast_to(rows[i][:, first + k:first + k + 1], (8, T)) for k in range(8)]
            m = multipliers(cs, True)
            w = jnp.where(in_block, 0.0, rows[i])
            for j in range(8):
                w = w - m[j] * vb[j]
            rows[i] = w
    cat = lambda x: jnp.concatenate(x, axis=0)
    return cat(lower), cat(upper), cat(pivots)

def factor_into(a_ref, l_ref, x_ref, n, lt_ref=None):
    steps = n // T
    def step(p, _):
        at = pl.ds(pl.multiple_of(p * T, T), T)
        low, up, piv = eliminate(a_ref[at, at])
        scale = lax.rsqrt(piv)
        xd = low * scale
        ld = up * scale
        x_ref[at, at] = xd
        l_ref[at, at] = ld.T
        for k in range(steps):
            @pl.when(p == k)
            def _():
                o = k * T
                e = o + T
                if k > 0:
                    part = dot_nn(l_ref[o:e, 0:o], x_ref[0:o, 0:o])
                    x_ref[o:e, 0:o] = -dot_nn(xd, part)
                if e < n:
                    x_ref[o:e, e:n] = jnp.zeros((T, n - e), jnp.float32)
                    l_ref[o:e, e:n] = jnp.zeros((T, n - e), jnp.float32)
                    l21 = dot_nt(a_ref[e:n, o:e], xd)
                    l_ref[e:n, o:e] = l21
                    a_ref[e:n, e:n] = a_ref[e:n, e:n] - dot_nt(l21, l21)
        return 0
    lax.fori_loop(0, steps, step, 0)


VMEM = pl.BlockSpec(memory_space=pltpu.VMEM)


def place():
    dof, snap = lax.axis_index("dof"), lax.axis_index("snap")
    core, y_hi = lax.rem(dof, 2), lax.rem(dof // 2, 2)
    return dof // 16, lax.rem(dof // 4, 4), y_hi * 2 + snap, core


def device(z, x, y, core):
    return (z * 16 + x * 4 + (y // 2) * 2 + core, lax.rem(y, 2))


def neighbours(with_y):
    z, x, y, core = place()
    over_core = [device(z, x, y, 1 - core)]
    over_x = [device(z, lax.rem(x + k, 4), y, core) for k in (1, 2, 3)]
    over_z = [device(lax.rem(z + k, 4), x, y, core) for k in (1, 2, 3)]
    down = device(z, x, lax.rem(y + 3, 4), core)
    greet = over_core + over_x + over_z
    if with_y:
        greet = greet + [down, device(z, x, lax.rem(y + 1, 4), core)]
    barrier = pltpu.get_barrier_semaphore()
    for partner in greet:
        pl.semaphore_signal(barrier, inc=1, device_id=partner, device_id_type=MESH)
    pl.semaphore_wait(barrier, len(greet))
    return over_core, over_x, over_z, down


class Sender:
    def __init__(self, send_sem, recv_sem):
        self.sems, self.used = (send_sem, recv_sem), 0

    def start(self, src, dst, to):
        send_sem, recv_sem = (s.at[self.used] for s in self.sems)
        self.used += 1
        copy = pltpu.make_async_remote_copy(
            src_ref=src, dst_ref=dst, send_sem=send_sem, recv_sem=recv_sem, device_id=to, device_id_type=MESH)
        copy.start()
        return copy

    def run(self, triples):
        for copy in [self.start(*t) for t in triples]:
            copy.wait()


def rows(start, size):
    return pl.ds(pl.multiple_of(start, size), size)


def scatter_sum(send, where, p_ref, half, quarter, rc, r1, r2, ry):
    over_core, over_x, over_z, down = where
    z, x, y, core = place()
    n = p_ref.shape[0]
    h, q, s, w = n // 2, n // 8, n // 32, n // 2
    left, right = pl.ds(0, w), pl.ds(w, w)
    send.run([(p_ref.at[rows((1 - core) * h, h)], rc, over_core[0])])
    half[...] = p_ref[rows(core * h, h), :] + rc[...]
    jobs = []
    for k in (2, 1, 3):
        jobs.append((half.at[rows(lax.rem(x + k, 4) * q, q), left], r1.at[0, k - 1], over_x[k - 1]))
        jobs.append((half.at[rows(lax.rem(z + k, 4) * q, q), right], r1.at[1, k - 1], over_z[k - 1]))
    send.run(jobs)
    quarter[0] = (half[rows(x * q, q), left] + r1[0, 1]) + (r1[0, 0] + r1[0, 2])
    quarter[1] = (half[rows(z * q, q), right] + r1[1, 1]) + (r1[1, 0] + r1[1, 2])
    jobs = []
    for k in (2, 1, 3):
        jobs.append((quarter.at[0, rows(lax.rem(z + k, 4) * s, s)], r2.at[0, k - 1], over_z[k - 1]))
        jobs.append((quarter.at[1, rows(lax.rem(x + k, 4) * s, s)], r2.at[1, k - 1], over_x[k - 1]))
    send.run(jobs)
    ry[y, 0] = (quarter[0, rows(z * s, s), :] + r2[0, 1]) + (r2[0, 0] + r2[0, 2])
    ry[y, 1] = (quarter[1, rows(x * s, s), :] + r2[1, 1]) + (r2[1, 0] + r2[1, 2])
    for k in (0, 1, 2):
        slot = ry.at[lax.rem(y + k, 4)]
        send.run([(slot, slot, down)])


def put_piece(out_ref, block, ry, slots):
    z, x, y, core = place()
    n = out_ref.shape[1]
    h, q, s, w = n // 2, n // 8, n // 32, n // 2
    at = (core * h + x * q + z * s, core * h + z * q + x * s)
    for side in (0, 1):
        total = ry[slots[0], side] + ry[slots[1], side]
        for i in range(2, len(slots), 2):
            total = total + (ry[slots[i], side] + ry[slots[i + 1], side])
        out_ref[block, rows(at[side], s), pl.ds(side * w, w)] = total


def gather_rows(send, where, out_ref):
    over_core, over_x, over_z, down = where
    z, x, y, core = place()
    n = out_ref.shape[1]
    h, q, s, w = n // 2, n // 8, n // 32, n // 2
    left, right = pl.ds(0, w), pl.ds(w, w)
    lpart = out_ref.at[:, rows(core * h + x * q + z * s, s), left]
    rpart = out_ref.at[:, rows(core * h + z * q + x * s, s), right]
    jobs = []
    for k in (2, 1, 3):
        jobs += [(lpart, lpart, over_z[k - 1]), (rpart, rpart, over_x[k - 1])]
    send.run(jobs)
    lpart = out_ref.at[:, rows(core * h + x * q, q), left]
    rpart = out_ref.at[:, rows(core * h + z * q, q), right]
    jobs = []
    for k in (2, 1, 3):
        jobs += [(lpart, lpart, over_x[k - 1]), (rpart, rpart, over_z[k - 1])]
    send.run(jobs)
    part = out_ref.at[:, rows(core * h, h)]
    send.run([(part, part, over_core[0])])


def split(x):
    high = x.astype(jnp.bfloat16)
    return high, (x - high.astype(jnp.float32)).astype(jnp.bfloat16)


def dot3(a, b, over):
    dims = ((over[:1], over[1:]), ((), ()))
    dot = lambda l, r: lax.dot_general(l, r, dims, preferred_element_type=jnp.float32)
    return dot(a[0], b[0]) + (dot(a[0], b[1]) + dot(a[1], b[0]))


CHUNK = 256
EARLY = 2
HALF = CHUNK // 2
CROSS = 8 * CHUNK + HALF
LEFT = 2
ROUND = 2


def dot_tn(a, b):
    return lax.dot_general(a, b, (((0,), (0,)), ((), ())), preferred_element_type=jnp.float32)


def thrice(x):
    high, low = split(x)
    return [high, high, low]


def weights(x):
    high, low = split(x)
    return jnp.concatenate([high, low, high], axis=1)


def whole_kernel(root, x_ref, own, factor_ref, got, w, relay, grams, la, xa, cross, lba, lb, xb, xba, acc,
                 half, quarter, rc, r1, r2, ry, half_b, quarter_b, rc_b, r1_b, r2_b, ry_b,
                 load_sem, go_sem, come_sem, hop_go_sem, hop_come_sem, send_sem, recv_sem):
    send = Sender(send_sem, recv_sem)
    snap = lax.axis_index("snap")
    first, second = snap == 0, snap == 1
    other = (lax.axis_index("dof"), 1 - snap)
    count, n = x_ref.shape
    chunks = count // CHUNK
    paired = chunks // 2
    direct = chunks - ROUND
    chunk = lambda c: pl.ds(pl.multiple_of(c * CHUNK, CHUNK), CHUNK)
    pair = lambda c: pl.ds(pl.multiple_of(c * 2 * CHUNK, 2 * CHUNK), 2 * CHUNK)

    def stream(c, base):
        return pltpu.make_async_remote_copy(
            src_ref=x_ref.at[pl.ds(pl.multiple_of(c * CHUNK + base, HALF), CHUNK)], dst_ref=got.at[chunk(c)],
            send_sem=go_sem.at[c], recv_sem=come_sem.at[c], device_id=other, device_id_type=MESH)

    def stream_half(start, base, sem):
        return pltpu.make_async_remote_copy(
            src_ref=x_ref.at[pl.ds(start + base, HALF)], dst_ref=got.at[pl.ds(start, HALF)],
            send_sem=go_sem.at[sem], recv_sem=come_sem.at[sem], device_id=other, device_id_type=MESH)

    a_halves = [stream_half(paired * CHUNK, 0, paired), stream_half(CROSS, 0, chunks)]
    last_b = stream_half((paired - 1) * CHUNK, CROSS, paired - 1)

    def loop(begin, end, body):
        def step(c, carry):
            body(c)
            return carry

        lax.fori_loop(begin, end, step, 0)

    load = lambda c: pltpu.make_async_copy(x_ref.at[chunk(c)], own.at[chunk(c)], load_sem.at[c])
    loop(0, chunks, lambda c: load(c).start())
    where = neighbours(True)
    down = where[3]

    def hop(which, i):
        src = (x_ref.at[chunk(direct + i)], relay.at[i], relay.at[i])[which]
        dst = (relay.at[i], relay.at[i], got.at[chunk(direct + i)])[which]
        go = hop_go_sem.at[i if which < 2 else ROUND + i]
        come = hop_come_sem.at[i] if which < 2 else come_sem.at[direct + i]
        return pltpu.make_async_remote_copy(
            src_ref=src, dst_ref=dst, send_sem=go, recv_sem=come, device_id=down, device_id_type=MESH)

    @pl.when(first)
    def _():
        loop(0, paired, lambda c: stream(c, 0).start())
        for copy in a_halves:
            copy.start()
        loop(paired + 1, direct, lambda c: stream(c, 0).start())

    @pl.when(second)
    def _():
        loop(0, EARLY, lambda c: stream(c, CROSS).start())
        last_b.start()

    acc[...] = jnp.zeros_like(acc)

    def gram_one(c):
        load(c).wait()
        high, low = split(own[chunk(c), :])
        acc[...] += dot_tn(high, high * jnp.bfloat16(0.5)) + dot_tn(high, low)

    loop(0, chunks, gram_one)
    acc[...] = acc[...] + acc[...].T

    scatter_sum(send, where, acc, half, quarter, rc, r1, r2, ry)
    put_piece(grams, 0, ry, (0, 2))
    put_piece(grams, 1, ry, (1, 3))

    @pl.when(second)
    def _():
        loop(EARLY, paired - 1, lambda c: stream(c, CROSS).start())

    @pl.when(first)
    def _():
        for i in range(ROUND):
            hop(0, i).start()

    gather_rows(send, where, grams)
    acc[...] = grams[0]
    factor_into(acc, la, xa, n)

    def basis_one(c, values, width):
        own[pair(c), :] = lax.dot_general(
            jnp.concatenate(values, axis=1), w[:, :width], (((1,), (1,)), ((), ())),
            preferred_element_type=jnp.float32)

    @pl.when(first)
    def _():
        w[:, :3 * n] = weights(xa[...] * root)
        factor_ref[:n, :] = la[...].T / root
        factor_ref[n:, :] = jnp.zeros((n, n), jnp.float32)

    acc[...] = jnp.zeros_like(acc)

    def add_cross(start, size, own_start):
        there = got[pl.ds(start, size), :]
        here = own[pl.ds(own_start, size), :]
        left = split(jnp.where(second, here, there))
        right = split(jnp.where(second, there, here))
        acc[...] += dot3(left, right, (0, 0))

    @pl.when(second)
    def _():
        hop(0, 0).wait_recv()
        hop(1, 0).start()

    def cross_one(c):
        stream(c, 0).wait_recv()
        start = pl.multiple_of(c * CHUNK, CHUNK)
        add_cross(start, CHUNK, pl.multiple_of(start + (1 - snap) * CROSS, HALF))

    loop(0, paired - 1, cross_one)
    tail = (paired - 1) * CHUNK

    @pl.when(first)
    def _():
        last_b.wait_recv()
        add_cross(tail, HALF, tail + CROSS)

    @pl.when(second)
    def _():
        stream(paired - 1, 0).wait_recv()
        add_cross(tail, CHUNK, tail)
        a_halves[0].wait_recv()
        add_cross(paired * CHUNK, HALF, paired * CHUNK)

    scatter_sum(send, where, acc, half_b, quarter_b, rc_b, r1_b, r2_b, ry_b)
    put_piece(cross, 0, ry_b, (0, 2, 1, 3))

    @pl.when(second)
    def _():
        for i in range(1, ROUND):
            hop(0, i).wait_recv()
            hop(1, i).start()

    @pl.when(first)
    def _():
        hop(1, 0).wait_recv()
        hop(2, 0).start()

    gather_rows(send, where, cross)

    @pl.when(first)
    def _():
        for i in range(1, ROUND):
            hop(1, i).wait_recv()
            hop(2, i).start()

    @pl.when(second)
    def _():
        lba[...] = dot_nt(cross[0], xa[...])
        acc[...] = grams[1] - dot_nt(lba[...], lba[...])
        factor_into(acc, lb, xb, n)
        xba[...] = -dot_nn(xb[...], dot_nn(lba[...], xa[...]))
        w[:, :3 * n] = weights(xb[...] * root)
        w[:, 3 * n:] = weights(xba[...] * root)
        factor_ref[:n, :] = lba[...].T / root
        factor_ref[n:, :] = lb[...].T / root

        def one(c):
            @pl.when(c > paired // 2)
            def _():
                stream(2 * c, 0).wait_recv()

            @pl.when(c >= paired // 2)
            def _():
                stream(2 * c + 1, 0).wait_recv()

            basis_one(c, thrice(own[pair(c), :]) + thrice(got[pair(c), :]), 6 * n)

        a_halves[1].wait_recv()
        loop(0, paired - LEFT, one)
        for c in range(2 * (paired - LEFT), chunks):
            stream(c, 0).wait_recv()
        loop(0, paired - 1, lambda c: stream(c, CROSS).wait_send())
        last_b.wait_send()
        for i in range(ROUND):
            hop(1, i).wait_send()

    @pl.when(first)
    def _():
        loop(0, paired - LEFT, lambda c: basis_one(c, thrice(own[pair(c), :]), 3 * n))
        loop(0, paired, lambda c: stream(c, 0).wait_send())
        for copy in a_halves:
            copy.wait_send()
        loop(paired + 1, direct, lambda c: stream(c, 0).wait_send())
        for i in range(ROUND):
            hop(0, i).wait_send()
            hop(2, i).wait_send()


def whole(snapshots, root):
    count, n = snapshots.shape
    chunks = count // CHUNK
    f32 = jnp.float32
    sums = [
        pltpu.VMEM((n // 2, n), f32),
        pltpu.VMEM((2, n // 8, n // 2), f32),
        pltpu.VMEM((n // 2, n), f32),
        pltpu.VMEM((2, 3, n // 8, n // 2), f32),
        pltpu.VMEM((2, 3, n // 32, n // 2), f32),
        pltpu.VMEM((4, 2, n // 32, n // 2), f32),
    ]
    square = pltpu.VMEM((n, n), f32)
    dma = pltpu.SemaphoreType.DMA
    return pl.pallas_call(
        functools.partial(whole_kernel, root),
        out_shape=(jax.ShapeDtypeStruct((count, n), f32), jax.ShapeDtypeStruct((2 * n, n), f32),
                   jax.ShapeDtypeStruct((count, n), f32), jax.ShapeDtypeStruct((n, 6 * n), jnp.bfloat16)),
        in_specs=[pl.BlockSpec(memory_space=pl.ANY)],
        out_specs=(VMEM,) * 4,
        scratch_shapes=[pltpu.VMEM((ROUND, CHUNK, n), f32)]
        + [pltpu.VMEM((2, n, n), f32), square, square, pltpu.VMEM((1, n, n), f32)] + [square] * 5
        + sums + sums
        + [dma((chunks,)), dma((chunks + 1,)), dma((chunks + 1,)), dma((2 * ROUND,)), dma((ROUND,)), dma((58,)), dma((58,))],
        compiler_params=pltpu.CompilerParams(
            collective_id=0, has_side_effects=True, vmem_limit_bytes=30 << 20),
        cost_estimate=pl.CostEstimate(flops=130 << 30, bytes_accessed=400 << 20, transcendentals=0),
    )(snapshots)


def finish_kernel(own, factor, got, w, basis_out, factor_out, stage, sems):
    count, n = own.shape
    size = 2 * CHUNK
    done = count - LEFT * size
    second = lax.axis_index("snap") == 1
    copies = [
        pltpu.make_async_copy(own.at[pl.ds(0, done)], basis_out.at[pl.ds(0, done)], sems.at[0]),
        pltpu.make_async_copy(factor, factor_out, sems.at[1]),
    ]
    for copy in copies:
        copy.start()
    for i in range(LEFT):
        at = pl.ds(done + i * size, size)

        def make(values, width):
            stage[i] = lax.dot_general(
                jnp.concatenate(values, axis=1), w[:, :width], (((1,), (1,)), ((), ())),
                preferred_element_type=jnp.float32)

        @pl.when(second)
        def _():
            make(thrice(own[at, :]) + thrice(got[at, :]), 6 * n)

        @pl.when(jnp.logical_not(second))
        def _():
            make(thrice(own[at, :]), 3 * n)

        copies.append(pltpu.make_async_copy(stage.at[i], basis_out.at[at], sems.at[2 + i]))
        copies[-1].start()
    for copy in copies:
        copy.wait()


def finish(own, factor, got, w):
    count, n = own.shape
    here = pl.BlockSpec(memory_space=pl.ANY)
    return pl.pallas_call(
        finish_kernel,
        out_shape=(jax.ShapeDtypeStruct(own.shape, own.dtype), jax.ShapeDtypeStruct(factor.shape, factor.dtype)),
        in_specs=[VMEM] * 4,
        out_specs=(here, here),
        scratch_shapes=[pltpu.VMEM((LEFT, 2 * CHUNK, n), jnp.float32), pltpu.SemaphoreType.DMA((2 + LEFT,))],
        compiler_params=pltpu.CompilerParams(vmem_limit_bytes=30 << 20),
    )(own, factor, got, w)


def on_device(snapshots):
    root_rows = float(snapshots.shape[0] * lax.axis_size("dof")) ** 0.5
    return tuple(finish(*whole(snapshots, root_rows)))


def solution(mesh):
    in_specs = (P("dof", "snap"),)
    out_specs = (P("dof", "snap"), P(None, "snap"))
    return jax.shard_map(
        on_device, mesh=mesh, in_specs=in_specs, out_specs=out_specs, check_vma=False
    )
```

```python
import functools

import jax
import jax.numpy as jnp
from jax import lax
from jax.experimental import pallas as pl
from jax.experimental.pallas import tpu as pltpu
from jax.sharding import PartitionSpec as P

MESH = pl.DeviceIdType.MESH
T = 128

def dot_nt(a, b):
    return dot4(split(a), split(b), (1, 1))


def dot_nn(a, b):
    return dot4(split(a), split(b), (1, 0))


def eliminate(block):
    sub = lax.broadcasted_iota(jnp.int32, (8, T), 0)
    lane = lax.broadcasted_iota(jnp.int32, (8, T), 1)
    rows = [block[8 * i:8 * i + 8, :] for i in range(T // 8)]
    upper, lower, pivots = [], [], []
    for b in range(T // 8):
        first = 8 * b
        in_block = (lane >= first) & (lane < first + 8)
        head = rows[b]
        cols = [jnp.broadcast_to(head[:, first + k:first + k + 1], (8, T)) for k in range(8)]
        t = {}
        for k in range(8):
            for j in range(k + 1):
                t[j, k] = jnp.broadcast_to(cols[k][j:j + 1, :], (8, T))
        recip = []
        for j in range(8):
            r = 1.0 / t[j, j]
            recip.append(r)
            for k in range(j + 1, 8):
                s = t[j, k] * r
                for l in range(k, 8):
                    t[k, l] = t[k, l] - s * t[j, l]
        pivot = t[0, 0]
        for j in range(1, 8):
            pivot = jnp.where(sub == j, t[j, j], pivot)
        pivots.append(pivot)

        def multipliers(cs, below):
            cs = list(cs)
            out = []
            for j in range(8):
                m = cs[j] * recip[j]
                if not below:
                    m = jnp.where(sub > j, m, 0.0)
                out.append(m)
                for k in range(j + 1, 8):
                    cs[k] = cs[k] - m * t[j, k]
            return out

        v = jnp.where(in_block, jnp.where(lane == sub + first, 1.0, 0.0), head)
        m = multipliers(cols, False)
        own = head
        for j in range(8):
            v = v - m[j] * jnp.broadcast_to(v[j:j + 1, :], (8, T))
            own = own - m[j] * jnp.broadcast_to(own[j:j + 1, :], (8, T))
        vb = [jnp.broadcast_to(v[j:j + 1, :], (8, T)) for j in range(8)]
        upper.append(jnp.where(lane >= sub + first, own, 0.0))
        lower.append(jnp.where(lane <= sub + first, v, 0.0))
        for i in range(b + 1, T // 8):
            cs = [jnp.broadcast_to(rows[i][:, first + k:first + k + 1], (8, T)) for k in range(8)]
            m = multipliers(cs, True)
            w = jnp.where(in_block, 0.0, rows[i])
            for j in range(8):
                w = w - m[j] * vb[j]
            rows[i] = w
    cat = lambda x: jnp.concatenate(x, axis=0)
    return cat(lower), cat(upper), cat(pivots)

def factor_into(a_ref, l_ref, x_ref, n, lt_ref=None):
    steps = n // T
    def step(p, _):
        at = pl.ds(pl.multiple_of(p * T, T), T)
        low, up, piv = eliminate(a_ref[at, at])
        scale = lax.rsqrt(piv)
        xd = low * scale
        ld = up * scale
        x_ref[at, at] = xd
        l_ref[at, at] = ld.T
        for k in range(steps):
            @pl.when(p == k)
            def _():
                o = k * T
                e = o + T
                if k > 0:
                    part = dot_nn(l_ref[o:e, 0:o], x_ref[0:o, 0:o])
                    x_ref[o:e, 0:o] = -dot_nn(xd, part)
                if e < n:
                    x_ref[o:e, e:n] = jnp.zeros((T, n - e), jnp.float32)
                    l_ref[o:e, e:n] = jnp.zeros((T, n - e), jnp.float32)
                    l21 = dot_nt(a_ref[e:n, o:e], xd)
                    l_ref[e:n, o:e] = l21
                    a_ref[e:n, e:n] = a_ref[e:n, e:n] - dot_nt(l21, l21)
        return 0
    lax.fori_loop(0, steps, step, 0)


VMEM = pl.BlockSpec(memory_space=pltpu.VMEM)


def place():
    dof, snap = lax.axis_index("dof"), lax.axis_index("snap")
    core, y_hi = lax.rem(dof, 2), lax.rem(dof // 2, 2)
    return dof // 16, lax.rem(dof // 4, 4), y_hi * 2 + snap, core


def device(z, x, y, core):
    return (z * 16 + x * 4 + (y // 2) * 2 + core, lax.rem(y, 2))


def neighbours(with_y):
    z, x, y, core = place()
    over_core = [device(z, x, y, 1 - core)]
    over_x = [device(z, lax.rem(x + k, 4), y, core) for k in (1, 2, 3)]
    over_z = [device(lax.rem(z + k, 4), x, y, core) for k in (1, 2, 3)]
    down = device(z, x, lax.rem(y + 3, 4), core)
    greet = over_core + over_x + over_z
    if with_y:
        greet = greet + [down, device(z, x, lax.rem(y + 1, 4), core)]
    barrier = pltpu.get_barrier_semaphore()
    for partner in greet:
        pl.semaphore_signal(barrier, inc=1, device_id=partner, device_id_type=MESH)
    pl.semaphore_wait(barrier, len(greet))
    return over_core, over_x, over_z, down


class Sender:
    def __init__(self, send_sem, recv_sem):
        self.sems, self.used = (send_sem, recv_sem), 0

    def start(self, src, dst, to):
        send_sem, recv_sem = (s.at[self.used] for s in self.sems)
        self.used += 1
        copy = pltpu.make_async_remote_copy(
            src_ref=src, dst_ref=dst, send_sem=send_sem, recv_sem=recv_sem, device_id=to, device_id_type=MESH)
        copy.start()
        return copy

    def run(self, triples):
        for copy in [self.start(*t) for t in triples]:
            copy.wait()


def rows(start, size):
    return pl.ds(pl.multiple_of(start, size), size)


def scatter_sum(send, where, p_ref, half, quarter, rc, r1, r2, ry):
    over_core, over_x, over_z, down = where
    z, x, y, core = place()
    n = p_ref.shape[0]
    h, q, s, w = n // 2, n // 8, n // 32, n // 2
    left, right = pl.ds(0, w), pl.ds(w, w)
    send.run([(p_ref.at[rows((1 - core) * h, h)], rc, over_core[0])])
    half[...] = p_ref[rows(core * h, h), :] + rc[...]
    jobs = []
    for k in (2, 1, 3):
        jobs.append((half.at[rows(lax.rem(x + k, 4) * q, q), left], r1.at[0, k - 1], over_x[k - 1]))
        jobs.append((half.at[rows(lax.rem(z + k, 4) * q, q), right], r1.at[1, k - 1], over_z[k - 1]))
    send.run(jobs)
    quarter[0] = (half[rows(x * q, q), left] + r1[0, 1]) + (r1[0, 0] + r1[0, 2])
    quarter[1] = (half[rows(z * q, q), right] + r1[1, 1]) + (r1[1, 0] + r1[1, 2])
    jobs = []
    for k in (2, 1, 3):
        jobs.append((quarter.at[0, rows(lax.rem(z + k, 4) * s, s)], r2.at[0, k - 1], over_z[k - 1]))
        jobs.append((quarter.at[1, rows(lax.rem(x + k, 4) * s, s)], r2.at[1, k - 1], over_x[k - 1]))
    send.run(jobs)
    ry[y, 0] = (quarter[0, rows(z * s, s), :] + r2[0, 1]) + (r2[0, 0] + r2[0, 2])
    ry[y, 1] = (quarter[1, rows(x * s, s), :] + r2[1, 1]) + (r2[1, 0] + r2[1, 2])
    for k in (0, 1, 2):
        slot = ry.at[lax.rem(y + k, 4)]
        send.run([(slot, slot, down)])


def put_piece(out_ref, block, ry, slots):
    z, x, y, core = place()
    n = out_ref.shape[1]
    h, q, s, w = n // 2, n // 8, n // 32, n // 2
    at = (core * h + x * q + z * s, core * h + z * q + x * s)
    for side in (0, 1):
        total = ry[slots[0], side] + ry[slots[1], side]
        for i in range(2, len(slots), 2):
            total = total + (ry[slots[i], side] + ry[slots[i + 1], side])
        out_ref[block, rows(at[side], s), pl.ds(side * w, w)] = total


def gather_rows(send, where, out_ref):
    over_core, over_x, over_z, down = where
    z, x, y, core = place()
    n = out_ref.shape[1]
    h, q, s, w = n // 2, n // 8, n // 32, n // 2
    left, right = pl.ds(0, w), pl.ds(w, w)
    lpart = out_ref.at[:, rows(core * h + x * q + z * s, s), left]
    rpart = out_ref.at[:, rows(core * h + z * q + x * s, s), right]
    jobs = []
    for k in (2, 1, 3):
        jobs += [(lpart, lpart, over_z[k - 1]), (rpart, rpart, over_x[k - 1])]
    send.run(jobs)
    block = (
        lambda k: out_ref.at[:, rows(core * h + lax.rem(x + k, 4) * q, q), left],
        lambda k: out_ref.at[:, rows(core * h + lax.rem(z + k, 4) * q, q), right],
    )
    landing = []
    for k in (1, 3, 2):
        for side, over in ((0, over_x), (1, over_z)):
            landing.append((send.start(block[side](0), block[side](0), over[k - 1]), side, k))
    passing = [send.start(block[side](0), block[side](0), over_core[0]) for side in (0, 1)]
    for copy, side, k in landing:
        copy.wait_recv()
        part = block[side](4 - k)
        passing.append(send.start(part, part, over_core[0]))
    for copy, _, _ in landing:
        copy.wait_send()
    for copy in passing:
        copy.wait()


def split(x):
    high = x.astype(jnp.bfloat16)
    return high, (x - high.astype(jnp.float32)).astype(jnp.bfloat16)


def dot4(a, b, over):
    dims = ((over[:1], over[1:]), ((), ()))
    dot = lambda l, r: lax.dot_general(l, r, dims, preferred_element_type=jnp.float32)
    return dot(a[0], b[0]) + (dot(a[0], b[1]) + (dot(a[1], b[0]) + dot(a[1], b[1])))


CHUNK = 256
EARLY = 2
HALF = CHUNK // 2
CROSS = 8 * CHUNK + HALF
LEFT = 2
ROUND = 2


def dot_tn(a, b):
    return lax.dot_general(a, b, (((0,), (0,)), ((), ())), preferred_element_type=jnp.float32)


def thrice(x):
    high, low = split(x)
    return [high, high, low]


def weights(x):
    high, low = split(x)
    return jnp.concatenate([high, low, high], axis=1)


def whole_kernel(root, x_ref, own, factor_ref, got, w, relay, grams, la, xa, cross, lba, lb, xb, xba, acc,
                 half, quarter, rc, r1, r2, ry, half_b, quarter_b, rc_b, r1_b, r2_b, ry_b,
                 load_sem, go_sem, come_sem, hop_go_sem, hop_come_sem, send_sem, recv_sem):
    send = Sender(send_sem, recv_sem)
    snap = lax.axis_index("snap")
    first, second = snap == 0, snap == 1
    other = (lax.axis_index("dof"), 1 - snap)
    count, n = x_ref.shape
    chunks = count // CHUNK
    paired = chunks // 2
    direct = chunks - ROUND
    chunk = lambda c: pl.ds(pl.multiple_of(c * CHUNK, CHUNK), CHUNK)
    pair = lambda c: pl.ds(pl.multiple_of(c * 2 * CHUNK, 2 * CHUNK), 2 * CHUNK)

    def stream(c, base):
        return pltpu.make_async_remote_copy(
            src_ref=x_ref.at[pl.ds(pl.multiple_of(c * CHUNK + base, HALF), CHUNK)], dst_ref=got.at[chunk(c)],
            send_sem=go_sem.at[c], recv_sem=come_sem.at[c], device_id=other, device_id_type=MESH)

    def stream_half(start, base, sem):
        return pltpu.make_async_remote_copy(
            src_ref=x_ref.at[pl.ds(start + base, HALF)], dst_ref=got.at[pl.ds(start, HALF)],
            send_sem=go_sem.at[sem], recv_sem=come_sem.at[sem], device_id=other, device_id_type=MESH)

    a_halves = [stream_half(paired * CHUNK, 0, paired), stream_half(CROSS, 0, chunks)]
    last_b = stream_half((paired - 1) * CHUNK, CROSS, paired - 1)

    def loop(begin, end, body):
        def step(c, carry):
            body(c)
            return carry

        lax.fori_loop(begin, end, step, 0)

    load = lambda c: pltpu.make_async_copy(x_ref.at[chunk(c)], own.at[chunk(c)], load_sem.at[c])
    loop(0, chunks, lambda c: load(c).start())
    where = neighbours(True)
    down = where[3]

    def hop(which, i):
        src = (x_ref.at[chunk(direct + i)], relay.at[i], relay.at[i])[which]
        dst = (relay.at[i], relay.at[i], got.at[chunk(direct + i)])[which]
        go = hop_go_sem.at[i if which < 2 else ROUND + i]
        come = hop_come_sem.at[i] if which < 2 else come_sem.at[direct + i]
        return pltpu.make_async_remote_copy(
            src_ref=src, dst_ref=dst, send_sem=go, recv_sem=come, device_id=down, device_id_type=MESH)

    @pl.when(first)
    def _():
        loop(0, paired, lambda c: stream(c, 0).start())
        for copy in a_halves:
            copy.start()
        loop(paired + 1, direct, lambda c: stream(c, 0).start())

    @pl.when(second)
    def _():
        loop(0, EARLY, lambda c: stream(c, CROSS).start())
        last_b.start()

    acc[...] = jnp.zeros_like(acc)

    def gram_one(c):
        load(c).wait()
        high, low = split(own[chunk(c), :])
        half_high, half_low = high * jnp.bfloat16(0.5), low * jnp.bfloat16(0.5)
        acc[...] += dot_tn(high, half_high) + dot_tn(high, low) + dot_tn(low, half_low)

    loop(0, chunks, gram_one)
    acc[...] = acc[...] + acc[...].T

    scatter_sum(send, where, acc, half, quarter, rc, r1, r2, ry)
    put_piece(grams, 0, ry, (0, 2))
    put_piece(grams, 1, ry, (1, 3))

    @pl.when(second)
    def _():
        loop(EARLY, paired - 1, lambda c: stream(c, CROSS).start())

    @pl.when(first)
    def _():
        for i in range(ROUND):
            hop(0, i).start()

    gather_rows(send, where, grams)
    acc[...] = grams[0]
    factor_into(acc, la, xa, n)

    def basis_one(c, values, width):
        own[pair(c), :] = lax.dot_general(
            jnp.concatenate(values, axis=1), w[:, :width], (((1,), (1,)), ((), ())),
            preferred_element_type=jnp.float32)

    @pl.when(first)
    def _():
        w[:, :3 * n] = weights(xa[...] * root)
        factor_ref[:n, :] = la[...].T / root
        factor_ref[n:, :] = jnp.zeros((n, n), jnp.float32)

    acc[...] = jnp.zeros_like(acc)

    def add_cross(start, size, own_start):
        there = got[pl.ds(start, size), :]
        here = own[pl.ds(own_start, size), :]
        left = split(jnp.where(second, here, there))
        right = split(jnp.where(second, there, here))
        acc[...] += dot4(left, right, (0, 0))

    @pl.when(second)
    def _():
        hop(0, 0).wait_recv()
        hop(1, 0).start()

    def cross_one(c):
        stream(c, 0).wait_recv()
        start = pl.multiple_of(c * CHUNK, CHUNK)
        add_cross(start, CHUNK, pl.multiple_of(start + (1 - snap) * CROSS, HALF))

    loop(0, paired - 1, cross_one)
    tail = (paired - 1) * CHUNK

    @pl.when(first)
    def _():
        last_b.wait_recv()
        add_cross(tail, HALF, tail + CROSS)

    @pl.when(second)
    def _():
        stream(paired - 1, 0).wait_recv()
        add_cross(tail, CHUNK, tail)
        a_halves[0].wait_recv()
        add_cross(paired * CHUNK, HALF, paired * CHUNK)

    scatter_sum(send, where, acc, half_b, quarter_b, rc_b, r1_b, r2_b, ry_b)
    put_piece(cross, 0, ry_b, (0, 2, 1, 3))

    @pl.when(second)
    def _():
        for i in range(1, ROUND):
            hop(0, i).wait_recv()
            hop(1, i).start()

    @pl.when(first)
    def _():
        hop(1, 0).wait_recv()
        hop(2, 0).start()

    gather_rows(send, where, cross)

    @pl.when(first)
    def _():
        for i in range(1, ROUND):
            hop(1, i).wait_recv()
            hop(2, i).start()

    @pl.when(second)
    def _():
        lba[...] = dot_nt(cross[0], xa[...])
        acc[...] = grams[1] - dot_nt(lba[...], lba[...])
        factor_into(acc, lb, xb, n)
        xba[...] = -dot_nn(xb[...], dot_nn(lba[...], xa[...]))
        w[:, :3 * n] = weights(xb[...] * root)
        w[:, 3 * n:] = weights(xba[...] * root)
        factor_ref[:n, :] = lba[...].T / root
        factor_ref[n:, :] = lb[...].T / root

        def one(c):
            @pl.when(c > paired // 2)
            def _():
                stream(2 * c, 0).wait_recv()

            @pl.when(c >= paired // 2)
            def _():
                stream(2 * c + 1, 0).wait_recv()

            basis_one(c, thrice(own[pair(c), :]) + thrice(got[pair(c), :]), 6 * n)

        a_halves[1].wait_recv()
        loop(0, paired - LEFT, one)
        for c in range(2 * (paired - LEFT), chunks):
            stream(c, 0).wait_recv()
        loop(0, paired - 1, lambda c: stream(c, CROSS).wait_send())
        last_b.wait_send()
        for i in range(ROUND):
            hop(1, i).wait_send()

    @pl.when(first)
    def _():
        loop(0, paired - LEFT, lambda c: basis_one(c, thrice(own[pair(c), :]), 3 * n))
        loop(0, paired, lambda c: stream(c, 0).wait_send())
        for copy in a_halves:
            copy.wait_send()
        loop(paired + 1, direct, lambda c: stream(c, 0).wait_send())
        for i in range(ROUND):
            hop(0, i).wait_send()
            hop(2, i).wait_send()


def whole(snapshots, root):
    count, n = snapshots.shape
    chunks = count // CHUNK
    f32 = jnp.float32
    sums = [
        pltpu.VMEM((n // 2, n), f32),
        pltpu.VMEM((2, n // 8, n // 2), f32),
        pltpu.VMEM((n // 2, n), f32),
        pltpu.VMEM((2, 3, n // 8, n // 2), f32),
        pltpu.VMEM((2, 3, n // 32, n // 2), f32),
        pltpu.VMEM((4, 2, n // 32, n // 2), f32),
    ]
    square = pltpu.VMEM((n, n), f32)
    dma = pltpu.SemaphoreType.DMA
    return pl.pallas_call(
        functools.partial(whole_kernel, root),
        out_shape=(jax.ShapeDtypeStruct((count, n), f32), jax.ShapeDtypeStruct((2 * n, n), f32),
                   jax.ShapeDtypeStruct((count, n), f32), jax.ShapeDtypeStruct((n, 6 * n), jnp.bfloat16)),
        in_specs=[pl.BlockSpec(memory_space=pl.ANY)],
        out_specs=(VMEM,) * 4,
        scratch_shapes=[pltpu.VMEM((ROUND, CHUNK, n), f32)]
        + [pltpu.VMEM((2, n, n), f32), square, square, pltpu.VMEM((1, n, n), f32)] + [square] * 5
        + sums + sums
        + [dma((chunks,)), dma((chunks + 1,)), dma((chunks + 1,)), dma((2 * ROUND,)), dma((ROUND,)), dma((72,)), dma((72,))],
        compiler_params=pltpu.CompilerParams(
            collective_id=0, has_side_effects=True, vmem_limit_bytes=30 << 20),
        cost_estimate=pl.CostEstimate(flops=130 << 30, bytes_accessed=400 << 20, transcendentals=0),
    )(snapshots)


def finish_kernel(own, factor, got, w, basis_out, factor_out, stage, sems):
    count, n = own.shape
    size = 2 * CHUNK
    done = count - LEFT * size
    second = lax.axis_index("snap") == 1
    copies = [
        pltpu.make_async_copy(own.at[pl.ds(0, done)], basis_out.at[pl.ds(0, done)], sems.at[0]),
        pltpu.make_async_copy(factor, factor_out, sems.at[1]),
    ]
    for copy in copies:
        copy.start()
    for i in range(LEFT):
        at = pl.ds(done + i * size, size)

        def make(values, width):
            stage[i] = lax.dot_general(
                jnp.concatenate(values, axis=1), w[:, :width], (((1,), (1,)), ((), ())),
                preferred_element_type=jnp.float32)

        @pl.when(second)
        def _():
            make(thrice(own[at, :]) + thrice(got[at, :]), 6 * n)

        @pl.when(jnp.logical_not(second))
        def _():
            make(thrice(own[at, :]), 3 * n)

        copies.append(pltpu.make_async_copy(stage.at[i], basis_out.at[at], sems.at[2 + i]))
        copies[-1].start()
    for copy in copies:
        copy.wait()


def finish(own, factor, got, w):
    count, n = own.shape
    here = pl.BlockSpec(memory_space=pl.ANY)
    return pl.pallas_call(
        finish_kernel,
        out_shape=(jax.ShapeDtypeStruct(own.shape, own.dtype), jax.ShapeDtypeStruct(factor.shape, factor.dtype)),
        in_specs=[VMEM] * 4,
        out_specs=(here, here),
        scratch_shapes=[pltpu.VMEM((LEFT, 2 * CHUNK, n), jnp.float32), pltpu.SemaphoreType.DMA((2 + LEFT,))],
        compiler_params=pltpu.CompilerParams(vmem_limit_bytes=30 << 20),
    )(own, factor, got, w)


def on_device(snapshots):
    root_rows = float(snapshots.shape[0] * lax.axis_size("dof")) ** 0.5
    return tuple(finish(*whole(snapshots, root_rows)))


def solution(mesh):
    in_specs = (P("dof", "snap"),)
    out_specs = (P("dof", "snap"), P(None, "snap"))
    return jax.shard_map(
        on_device, mesh=mesh, in_specs=in_specs, out_specs=out_specs, check_vma=False
    )
```

```python
import functools

import jax
import jax.numpy as jnp
from jax import lax
from jax.experimental import pallas as pl
from jax.experimental.pallas import tpu as pltpu
from jax.sharding import PartitionSpec as P

MESH = pl.DeviceIdType.MESH
T = 128

def dot_nt(a, b):
    return dot4(split(a), split(b), (1, 1))


def dot_nn(a, b):
    return dot4(split(a), split(b), (1, 0))


def eliminate(block):
    sub = lax.broadcasted_iota(jnp.int32, (8, T), 0)
    lane = lax.broadcasted_iota(jnp.int32, (8, T), 1)
    rows = [block[8 * i:8 * i + 8, :] for i in range(T // 8)]
    upper, lower, pivots = [], [], []
    for b in range(T // 8):
        first = 8 * b
        in_block = (lane >= first) & (lane < first + 8)
        head = rows[b]
        cols = [jnp.broadcast_to(head[:, first + k:first + k + 1], (8, T)) for k in range(8)]
        t = {}
        for k in range(8):
            for j in range(k + 1):
                t[j, k] = jnp.broadcast_to(cols[k][j:j + 1, :], (8, T))
        recip = []
        for j in range(8):
            r = 1.0 / t[j, j]
            recip.append(r)
            for k in range(j + 1, 8):
                s = t[j, k] * r
                for l in range(k, 8):
                    t[k, l] = t[k, l] - s * t[j, l]
        pivot = t[0, 0]
        for j in range(1, 8):
            pivot = jnp.where(sub == j, t[j, j], pivot)
        pivots.append(pivot)

        def multipliers(cs, below):
            cs = list(cs)
            out = []
            for j in range(8):
                m = cs[j] * recip[j]
                if not below:
                    m = jnp.where(sub > j, m, 0.0)
                out.append(m)
                for k in range(j + 1, 8):
                    cs[k] = cs[k] - m * t[j, k]
            return out

        v = jnp.where(in_block, jnp.where(lane == sub + first, 1.0, 0.0), head)
        m = multipliers(cols, False)
        own = head
        for j in range(8):
            v = v - m[j] * jnp.broadcast_to(v[j:j + 1, :], (8, T))
            own = own - m[j] * jnp.broadcast_to(own[j:j + 1, :], (8, T))
        vb = [jnp.broadcast_to(v[j:j + 1, :], (8, T)) for j in range(8)]
        upper.append(jnp.where(lane >= sub + first, own, 0.0))
        lower.append(jnp.where(lane <= sub + first, v, 0.0))
        for i in range(b + 1, T // 8):
            cs = [jnp.broadcast_to(rows[i][:, first + k:first + k + 1], (8, T)) for k in range(8)]
            m = multipliers(cs, True)
            w = jnp.where(in_block, 0.0, rows[i])
            for j in range(8):
                w = w - m[j] * vb[j]
            rows[i] = w
    cat = lambda x: jnp.concatenate(x, axis=0)
    return cat(lower), cat(upper), cat(pivots)

def factor_into(a_ref, l_ref, x_ref, n, lt_ref=None):
    steps = n // T
    def step(p, _):
        at = pl.ds(pl.multiple_of(p * T, T), T)
        low, up, piv = eliminate(a_ref[at, at])
        scale = lax.rsqrt(piv)
        xd = low * scale
        ld = up * scale
        x_ref[at, at] = xd
        l_ref[at, at] = ld.T
        for k in range(steps):
            @pl.when(p == k)
            def _():
                o = k * T
                e = o + T
                if k > 0:
                    part = dot_nn(l_ref[o:e, 0:o], x_ref[0:o, 0:o])
                    x_ref[o:e, 0:o] = -dot_nn(xd, part)
                if e < n:
                    x_ref[o:e, e:n] = jnp.zeros((T, n - e), jnp.float32)
                    l_ref[o:e, e:n] = jnp.zeros((T, n - e), jnp.float32)
                    l21 = dot_nt(a_ref[e:n, o:e], xd)
                    l_ref[e:n, o:e] = l21
                    a_ref[e:n, e:n] = a_ref[e:n, e:n] - dot_nt(l21, l21)
        return 0
    lax.fori_loop(0, steps, step, 0)


VMEM = pl.BlockSpec(memory_space=pltpu.VMEM)


def place():
    dof, snap = lax.axis_index("dof"), lax.axis_index("snap")
    core, y_hi = lax.rem(dof, 2), lax.rem(dof // 2, 2)
    return dof // 16, lax.rem(dof // 4, 4), y_hi * 2 + snap, core


def device(z, x, y, core):
    return (z * 16 + x * 4 + (y // 2) * 2 + core, lax.rem(y, 2))


def neighbours(with_y):
    z, x, y, core = place()
    over_core = [device(z, x, y, 1 - core)]
    over_x = [device(z, lax.rem(x + k, 4), y, core) for k in (1, 2, 3)]
    over_z = [device(lax.rem(z + k, 4), x, y, core) for k in (1, 2, 3)]
    down = device(z, x, lax.rem(y + 3, 4), core)
    greet = over_core + over_x + over_z
    if with_y:
        greet = greet + [down, device(z, x, lax.rem(y + 1, 4), core)]
    barrier = pltpu.get_barrier_semaphore()
    for partner in greet:
        pl.semaphore_signal(barrier, inc=1, device_id=partner, device_id_type=MESH)
    pl.semaphore_wait(barrier, len(greet))
    return over_core, over_x, over_z, down


class Sender:
    def __init__(self, send_sem, recv_sem):
        self.sems, self.used = (send_sem, recv_sem), 0

    def start(self, src, dst, to):
        send_sem, recv_sem = (s.at[self.used] for s in self.sems)
        self.used += 1
        copy = pltpu.make_async_remote_copy(
            src_ref=src, dst_ref=dst, send_sem=send_sem, recv_sem=recv_sem, device_id=to, device_id_type=MESH)
        copy.start()
        return copy

    def run(self, triples):
        for copy in [self.start(*t) for t in triples]:
            copy.wait()


def rows(start, size):
    return pl.ds(pl.multiple_of(start, size), size)


def scatter_sum(send, where, p_ref, half, quarter, rc, r1, r2, ry, behind):
    over_core, over_x, over_z, down = where
    z, x, y, core = place()
    n = p_ref.shape[0]
    h, q, s, w = n // 2, n // 8, n // 32, n // 2
    left, right = pl.ds(0, w), pl.ds(w, w)
    send.run([(p_ref.at[rows((1 - core) * h, h)], rc, over_core[0])])
    half[...] = p_ref[rows(core * h, h), :] + rc[...]
    jobs = []
    for k in (2, 1, 3):
        jobs.append((half.at[rows(lax.rem(x + k, 4) * q, q), left], r1.at[0, k - 1], over_x[k - 1]))
        jobs.append((half.at[rows(lax.rem(z + k, 4) * q, q), right], r1.at[1, k - 1], over_z[k - 1]))
    send.run(jobs)
    quarter[0] = (half[rows(x * q, q), left] + r1[0, 1]) + (r1[0, 0] + r1[0, 2])
    quarter[1] = (half[rows(z * q, q), right] + r1[1, 1]) + (r1[1, 0] + r1[1, 2])
    jobs = []
    for k in (2, 1, 3):
        jobs.append((quarter.at[0, rows(lax.rem(z + k, 4) * s, s)], r2.at[0, k - 1], over_z[k - 1]))
        jobs.append((quarter.at[1, rows(lax.rem(x + k, 4) * s, s)], r2.at[1, k - 1], over_x[k - 1]))
    send.run(jobs)
    ry[y, 0] = (quarter[0, rows(z * s, s), :] + r2[0, 1]) + (r2[0, 0] + r2[0, 2])
    ry[y, 1] = (quarter[1, rows(x * s, s), :] + r2[1, 1]) + (r2[1, 0] + r2[1, 2])
    for k in (0, 1, 2):
        slot = ry.at[lax.rem(y + k, 4)]
        copy = send.start(slot, slot, down)
        if k == 2:
            behind()
        copy.wait()


def put_piece(out_ref, block, ry, slots):
    z, x, y, core = place()
    n = out_ref.shape[1]
    h, q, s, w = n // 2, n // 8, n // 32, n // 2
    at = (core * h + x * q + z * s, core * h + z * q + x * s)
    for side in (0, 1):
        total = ry[slots[0], side] + ry[slots[1], side]
        for i in range(2, len(slots), 2):
            total = total + (ry[slots[i], side] + ry[slots[i + 1], side])
        out_ref[block, rows(at[side], s), pl.ds(side * w, w)] = total


def gather_rows(send, where, out_ref):
    over_core, over_x, over_z, down = where
    z, x, y, core = place()
    n = out_ref.shape[1]
    h, q, s, w = n // 2, n // 8, n // 32, n // 2
    left, right = pl.ds(0, w), pl.ds(w, w)
    lpart = out_ref.at[:, rows(core * h + x * q + z * s, s), left]
    rpart = out_ref.at[:, rows(core * h + z * q + x * s, s), right]
    jobs = []
    for k in (2, 1, 3):
        jobs += [(lpart, lpart, over_z[k - 1]), (rpart, rpart, over_x[k - 1])]
    send.run(jobs)
    block = (
        lambda k: out_ref.at[:, rows(core * h + lax.rem(x + k, 4) * q, q), left],
        lambda k: out_ref.at[:, rows(core * h + lax.rem(z + k, 4) * q, q), right],
    )
    landing = []
    for k in (1, 3, 2):
        for side, over in ((0, over_x), (1, over_z)):
            landing.append((send.start(block[side](0), block[side](0), over[k - 1]), side, k))
    passing = [send.start(block[side](0), block[side](0), over_core[0]) for side in (0, 1)]
    for copy, side, k in landing:
        copy.wait_recv()
        part = block[side](4 - k)
        passing.append(send.start(part, part, over_core[0]))
    for copy, _, _ in landing:
        copy.wait_send()
    for copy in passing:
        copy.wait()


def split(x):
    high = x.astype(jnp.bfloat16)
    return high, (x - high.astype(jnp.float32)).astype(jnp.bfloat16)


def dot4(a, b, over):
    dims = ((over[:1], over[1:]), ((), ()))
    dot = lambda l, r: lax.dot_general(l, r, dims, preferred_element_type=jnp.float32)
    return dot(a[0], b[0]) + (dot(a[0], b[1]) + (dot(a[1], b[0]) + dot(a[1], b[1])))


CHUNK = 256
EARLY = 2
PART = CHUNK // 4
CROSS = 8 * CHUNK + PART
LEFT = 2
ROUND = 2


def dot_tn(a, b):
    return lax.dot_general(a, b, (((0,), (0,)), ((), ())), preferred_element_type=jnp.float32)


def thrice(x):
    high, low = split(x)
    return [high, high, low]


def weights(x):
    high, low = split(x)
    return jnp.concatenate([high, low, high], axis=1)


def whole_kernel(root, x_ref, own, factor_ref, got, w, relay, grams, la, xa, cross, lba, lb, xb, xba, acc,
                 half, quarter, rc, r1, r2, ry, half_b, quarter_b, rc_b, r1_b, r2_b, ry_b,
                 load_sem, go_sem, come_sem, hop_go_sem, hop_come_sem, send_sem, recv_sem):
    send = Sender(send_sem, recv_sem)
    snap = lax.axis_index("snap")
    first, second = snap == 0, snap == 1
    other = (lax.axis_index("dof"), 1 - snap)
    count, n = x_ref.shape
    chunks = count // CHUNK
    paired = chunks // 2
    direct = chunks - ROUND
    chunk = lambda c: pl.ds(pl.multiple_of(c * CHUNK, CHUNK), CHUNK)
    pair = lambda c: pl.ds(pl.multiple_of(c * 2 * CHUNK, 2 * CHUNK), 2 * CHUNK)

    def stream(c, base):
        return pltpu.make_async_remote_copy(
            src_ref=x_ref.at[pl.ds(pl.multiple_of(c * CHUNK + base, PART), CHUNK)], dst_ref=got.at[chunk(c)],
            send_sem=go_sem.at[c], recv_sem=come_sem.at[c], device_id=other, device_id_type=MESH)

    def stream_part(start, base, size, sem):
        return pltpu.make_async_remote_copy(
            src_ref=x_ref.at[pl.ds(start + base, size)], dst_ref=got.at[pl.ds(start, size)],
            send_sem=go_sem.at[sem], recv_sem=come_sem.at[sem], device_id=other, device_id_type=MESH)

    a_parts = [stream_part(paired * CHUNK, 0, PART, paired), stream_part(CROSS, 0, CHUNK - PART, chunks)]
    last_b = stream_part((paired - 1) * CHUNK, CROSS, CHUNK - PART, paired - 1)

    def loop(begin, end, body):
        def step(c, carry):
            body(c)
            return carry

        lax.fori_loop(begin, end, step, 0)

    load = lambda c: pltpu.make_async_copy(x_ref.at[chunk(c)], own.at[chunk(c)], load_sem.at[c])
    loop(0, chunks, lambda c: load(c).start())
    where = neighbours(True)
    down = where[3]

    def hop(which, i):
        src = (x_ref.at[chunk(direct + i)], relay.at[i], relay.at[i])[which]
        dst = (relay.at[i], relay.at[i], got.at[chunk(direct + i)])[which]
        go = hop_go_sem.at[i if which < 2 else ROUND + i]
        come = hop_come_sem.at[i] if which < 2 else come_sem.at[direct + i]
        return pltpu.make_async_remote_copy(
            src_ref=src, dst_ref=dst, send_sem=go, recv_sem=come, device_id=down, device_id_type=MESH)

    @pl.when(first)
    def _():
        loop(0, paired, lambda c: stream(c, 0).start())
        for copy in a_parts:
            copy.start()
        loop(paired + 1, direct, lambda c: stream(c, 0).start())

    @pl.when(second)
    def _():
        loop(0, EARLY, lambda c: stream(c, CROSS).start())
        last_b.start()

    acc[...] = jnp.zeros_like(acc)

    def gram_one(c):
        load(c).wait()
        high, low = split(own[chunk(c), :])
        half_high, half_low = high * jnp.bfloat16(0.5), low * jnp.bfloat16(0.5)
        acc[...] += dot_tn(high, half_high) + dot_tn(high, low) + dot_tn(low, half_low)

    loop(0, chunks, gram_one)
    acc[...] = acc[...] + acc[...].T

    def behind_first():
        @pl.when(second)
        def _():
            loop(EARLY, paired - 1, lambda c: stream(c, CROSS).start())

        @pl.when(first)
        def _():
            for i in range(ROUND):
                hop(0, i).start()

    scatter_sum(send, where, acc, half, quarter, rc, r1, r2, ry, behind_first)
    put_piece(grams, 0, ry, (0, 2))
    put_piece(grams, 1, ry, (1, 3))
    gather_rows(send, where, grams)
    acc[...] = grams[0]
    factor_into(acc, la, xa, n)

    def basis_one(c, values, width):
        own[pair(c), :] = lax.dot_general(
            jnp.concatenate(values, axis=1), w[:, :width], (((1,), (1,)), ((), ())),
            preferred_element_type=jnp.float32)

    @pl.when(first)
    def _():
        w[:, :3 * n] = weights(xa[...] * root)
        factor_ref[:n, :] = la[...].T / root
        factor_ref[n:, :] = jnp.zeros((n, n), jnp.float32)

    acc[...] = jnp.zeros_like(acc)

    def add_cross(start, size, own_start):
        there = got[pl.ds(start, size), :]
        here = own[pl.ds(own_start, size), :]
        left = split(jnp.where(second, here, there))
        right = split(jnp.where(second, there, here))
        acc[...] += dot4(left, right, (0, 0))

    @pl.when(second)
    def _():
        hop(0, 0).wait_recv()
        hop(1, 0).start()

    def cross_one(c):
        stream(c, 0).wait_recv()
        start = pl.multiple_of(c * CHUNK, CHUNK)
        add_cross(start, CHUNK, pl.multiple_of(start + (1 - snap) * CROSS, PART))

    loop(0, paired - 1, cross_one)
    tail = (paired - 1) * CHUNK

    @pl.when(first)
    def _():
        last_b.wait_recv()
        add_cross(tail, CHUNK - PART, tail + CROSS)

    @pl.when(second)
    def _():
        stream(paired - 1, 0).wait_recv()
        add_cross(tail, CHUNK, tail)
        a_parts[0].wait_recv()
        add_cross(paired * CHUNK, PART, paired * CHUNK)

    def behind_second():
        @pl.when(second)
        def _():
            for i in range(1, ROUND):
                hop(0, i).wait_recv()
                hop(1, i).start()

        @pl.when(first)
        def _():
            hop(1, 0).wait_recv()
            hop(2, 0).start()

    scatter_sum(send, where, acc, half_b, quarter_b, rc_b, r1_b, r2_b, ry_b, behind_second)
    put_piece(cross, 0, ry_b, (0, 2, 1, 3))
    gather_rows(send, where, cross)

    @pl.when(first)
    def _():
        for i in range(1, ROUND):
            hop(1, i).wait_recv()
            hop(2, i).start()

    @pl.when(second)
    def _():
        lba[...] = dot_nt(cross[0], xa[...])
        acc[...] = grams[1] - dot_nt(lba[...], lba[...])
        factor_into(acc, lb, xb, n)
        xba[...] = -dot_nn(xb[...], dot_nn(lba[...], xa[...]))
        w[:, :3 * n] = weights(xb[...] * root)
        w[:, 3 * n:] = weights(xba[...] * root)
        factor_ref[:n, :] = lba[...].T / root
        factor_ref[n:, :] = lb[...].T / root

        def one(c):
            @pl.when(c > paired // 2)
            def _():
                stream(2 * c, 0).wait_recv()

            @pl.when(c >= paired // 2)
            def _():
                stream(2 * c + 1, 0).wait_recv()

            basis_one(c, thrice(own[pair(c), :]) + thrice(got[pair(c), :]), 6 * n)

        a_parts[1].wait_recv()
        loop(0, paired - LEFT, one)
        for c in range(2 * (paired - LEFT), chunks):
            stream(c, 0).wait_recv()
        loop(0, paired - 1, lambda c: stream(c, CROSS).wait_send())
        last_b.wait_send()
        for i in range(ROUND):
            hop(1, i).wait_send()

    @pl.when(first)
    def _():
        loop(0, paired - LEFT, lambda c: basis_one(c, thrice(own[pair(c), :]), 3 * n))
        loop(0, paired, lambda c: stream(c, 0).wait_send())
        for copy in a_parts:
            copy.wait_send()
        loop(paired + 1, direct, lambda c: stream(c, 0).wait_send())
        for i in range(ROUND):
            hop(0, i).wait_send()
            hop(2, i).wait_send()


def whole(snapshots, root):
    count, n = snapshots.shape
    chunks = count // CHUNK
    f32 = jnp.float32
    sums = [
        pltpu.VMEM((n // 2, n), f32),
        pltpu.VMEM((2, n // 8, n // 2), f32),
        pltpu.VMEM((n // 2, n), f32),
        pltpu.VMEM((2, 3, n // 8, n // 2), f32),
        pltpu.VMEM((2, 3, n // 32, n // 2), f32),
        pltpu.VMEM((4, 2, n // 32, n // 2), f32),
    ]
    square = pltpu.VMEM((n, n), f32)
    dma = pltpu.SemaphoreType.DMA
    return pl.pallas_call(
        functools.partial(whole_kernel, root),
        out_shape=(jax.ShapeDtypeStruct((count, n), f32), jax.ShapeDtypeStruct((2 * n, n), f32),
                   jax.ShapeDtypeStruct((count, n), f32), jax.ShapeDtypeStruct((n, 6 * n), jnp.bfloat16)),
        in_specs=[pl.BlockSpec(memory_space=pl.ANY)],
        out_specs=(VMEM,) * 4,
        scratch_shapes=[pltpu.VMEM((ROUND, CHUNK, n), f32)]
        + [pltpu.VMEM((2, n, n), f32), square, square, pltpu.VMEM((1, n, n), f32)] + [square] * 5
        + sums + sums
        + [dma((chunks,)), dma((chunks + 1,)), dma((chunks + 1,)), dma((2 * ROUND,)), dma((ROUND,)), dma((72,)), dma((72,))],
        compiler_params=pltpu.CompilerParams(
            collective_id=0, has_side_effects=True, vmem_limit_bytes=30 << 20),
        cost_estimate=pl.CostEstimate(flops=130 << 30, bytes_accessed=400 << 20, transcendentals=0),
    )(snapshots)


def finish_kernel(own, factor, got, w, basis_out, factor_out, stage, sems):
    count, n = own.shape
    size = 2 * CHUNK
    done = count - LEFT * size
    second = lax.axis_index("snap") == 1
    copies = [
        pltpu.make_async_copy(own.at[pl.ds(0, done)], basis_out.at[pl.ds(0, done)], sems.at[0]),
        pltpu.make_async_copy(factor, factor_out, sems.at[1]),
    ]
    for copy in copies:
        copy.start()
    for i in range(LEFT):
        at = pl.ds(done + i * size, size)

        def make(values, width):
            stage[i] = lax.dot_general(
                jnp.concatenate(values, axis=1), w[:, :width], (((1,), (1,)), ((), ())),
                preferred_element_type=jnp.float32)

        @pl.when(second)
        def _():
            make(thrice(own[at, :]) + thrice(got[at, :]), 6 * n)

        @pl.when(jnp.logical_not(second))
        def _():
            make(thrice(own[at, :]), 3 * n)

        copies.append(pltpu.make_async_copy(stage.at[i], basis_out.at[at], sems.at[2 + i]))
        copies[-1].start()
    for copy in copies:
        copy.wait()


def finish(own, factor, got, w):
    count, n = own.shape
    here = pl.BlockSpec(memory_space=pl.ANY)
    return pl.pallas_call(
        finish_kernel,
        out_shape=(jax.ShapeDtypeStruct(own.shape, own.dtype), jax.ShapeDtypeStruct(factor.shape, factor.dtype)),
        in_specs=[VMEM] * 4,
        out_specs=(here, here),
        scratch_shapes=[pltpu.VMEM((LEFT, 2 * CHUNK, n), jnp.float32), pltpu.SemaphoreType.DMA((2 + LEFT,))],
        compiler_params=pltpu.CompilerParams(vmem_limit_bytes=30 << 20),
    )(own, factor, got, w)


def on_device(snapshots):
    root_rows = float(snapshots.shape[0] * lax.axis_size("dof")) ** 0.5
    return tuple(finish(*whole(snapshots, root_rows)))


def solution(mesh):
    in_specs = (P("dof", "snap"),)
    out_specs = (P("dof", "snap"), P(None, "snap"))
    return jax.shard_map(
        on_device, mesh=mesh, in_specs=in_specs, out_specs=out_specs, check_vma=False
    )
```

```python
import functools

import jax
import jax.numpy as jnp
from jax import lax
from jax.experimental import pallas as pl
from jax.experimental.pallas import tpu as pltpu
from jax.sharding import PartitionSpec as P

MESH = pl.DeviceIdType.MESH
T = 128

def dot_nt(a, b):
    return dot4(split(a), split(b), (1, 1))


def dot_nn(a, b):
    return dot4(split(a), split(b), (1, 0))


def eliminate(block):
    sub = lax.broadcasted_iota(jnp.int32, (8, T), 0)
    lane = lax.broadcasted_iota(jnp.int32, (8, T), 1)
    rows = [block[8 * i:8 * i + 8, :] for i in range(T // 8)]
    upper, lower, pivots = [], [], []
    for b in range(T // 8):
        first = 8 * b
        in_block = (lane >= first) & (lane < first + 8)
        head = rows[b]
        cols = [jnp.broadcast_to(head[:, first + k:first + k + 1], (8, T)) for k in range(8)]
        t = {}
        for k in range(8):
            for j in range(k + 1):
                t[j, k] = jnp.broadcast_to(cols[k][j:j + 1, :], (8, T))
        recip = []
        for j in range(8):
            r = 1.0 / t[j, j]
            recip.append(r)
            for k in range(j + 1, 8):
                s = t[j, k] * r
                for l in range(k, 8):
                    t[k, l] = t[k, l] - s * t[j, l]
        pivot = t[0, 0]
        for j in range(1, 8):
            pivot = jnp.where(sub == j, t[j, j], pivot)
        pivots.append(pivot)

        def multipliers(cs, below):
            cs = list(cs)
            out = []
            for j in range(8):
                m = cs[j] * recip[j]
                if not below:
                    m = jnp.where(sub > j, m, 0.0)
                out.append(m)
                for k in range(j + 1, 8):
                    cs[k] = cs[k] - m * t[j, k]
            return out

        v = jnp.where(in_block, jnp.where(lane == sub + first, 1.0, 0.0), head)
        m = multipliers(cols, False)
        own = head
        for j in range(8):
            v = v - m[j] * jnp.broadcast_to(v[j:j + 1, :], (8, T))
            own = own - m[j] * jnp.broadcast_to(own[j:j + 1, :], (8, T))
        vb = [jnp.broadcast_to(v[j:j + 1, :], (8, T)) for j in range(8)]
        upper.append(jnp.where(lane >= sub + first, own, 0.0))
        lower.append(jnp.where(lane <= sub + first, v, 0.0))
        for i in range(b + 1, T // 8):
            cs = [jnp.broadcast_to(rows[i][:, first + k:first + k + 1], (8, T)) for k in range(8)]
            m = multipliers(cs, True)
            w = jnp.where(in_block, 0.0, rows[i])
            for j in range(8):
                w = w - m[j] * vb[j]
            rows[i] = w
    cat = lambda x: jnp.concatenate(x, axis=0)
    return cat(lower), cat(upper), cat(pivots)

def factor_into(a_ref, l_ref, x_ref, n, lt_ref=None):
    steps = n // T
    def step(p, _):
        at = pl.ds(pl.multiple_of(p * T, T), T)
        low, up, piv = eliminate(a_ref[at, at])
        scale = lax.rsqrt(piv)
        xd = low * scale
        ld = up * scale
        x_ref[at, at] = xd
        l_ref[at, at] = ld.T
        for k in range(steps):
            @pl.when(p == k)
            def _():
                o = k * T
                e = o + T
                if k > 0:
                    part = dot_nn(l_ref[o:e, 0:o], x_ref[0:o, 0:o])
                    x_ref[o:e, 0:o] = -dot_nn(xd, part)
                if e < n:
                    x_ref[o:e, e:n] = jnp.zeros((T, n - e), jnp.float32)
                    l_ref[o:e, e:n] = jnp.zeros((T, n - e), jnp.float32)
                    l21 = dot_nt(a_ref[e:n, o:e], xd)
                    l_ref[e:n, o:e] = l21
                    a_ref[e:n, e:n] = a_ref[e:n, e:n] - dot_nt(l21, l21)
        return 0
    lax.fori_loop(0, steps, step, 0)


VMEM = pl.BlockSpec(memory_space=pltpu.VMEM)


def place():
    dof, snap = lax.axis_index("dof"), lax.axis_index("snap")
    core, y_hi = lax.rem(dof, 2), lax.rem(dof // 2, 2)
    return dof // 16, lax.rem(dof // 4, 4), y_hi * 2 + snap, core


def device(z, x, y, core):
    return (z * 16 + x * 4 + (y // 2) * 2 + core, lax.rem(y, 2))


def neighbours(with_y):
    z, x, y, core = place()
    over_core = [device(z, x, y, 1 - core)]
    over_x = [device(z, lax.rem(x + k, 4), y, core) for k in (1, 2, 3)]
    over_z = [device(lax.rem(z + k, 4), x, y, core) for k in (1, 2, 3)]
    down = device(z, x, lax.rem(y + 3, 4), core)
    greet = over_core + over_x + over_z
    if with_y:
        greet = greet + [down, device(z, x, lax.rem(y + 1, 4), core)]
    barrier = pltpu.get_barrier_semaphore()
    for partner in greet:
        pl.semaphore_signal(barrier, inc=1, device_id=partner, device_id_type=MESH)
    pl.semaphore_wait(barrier, len(greet))
    return over_core, over_x, over_z, down


class Sender:
    def __init__(self, send_sem, recv_sem):
        self.sems, self.used = (send_sem, recv_sem), 0

    def start(self, src, dst, to):
        send_sem, recv_sem = (s.at[self.used] for s in self.sems)
        self.used += 1
        copy = pltpu.make_async_remote_copy(
            src_ref=src, dst_ref=dst, send_sem=send_sem, recv_sem=recv_sem, device_id=to, device_id_type=MESH)
        copy.start()
        return copy

    def run(self, triples):
        for copy in [self.start(*t) for t in triples]:
            copy.wait()


def rows(start, size):
    return pl.ds(pl.multiple_of(start, size), size)


def scatter_sum(send, where, p_ref, half, quarter, rc, r1, r2, ry, behind):
    over_core, over_x, over_z, down = where
    z, x, y, core = place()
    n = p_ref.shape[0]
    h, q, s, w = n // 2, n // 8, n // 32, n // 2
    left, right = pl.ds(0, w), pl.ds(w, w)
    send.run([(p_ref.at[rows((1 - core) * h, h)], rc, over_core[0])])
    half[...] = p_ref[rows(core * h, h), :] + rc[...]
    jobs = []
    for k in (2, 1, 3):
        jobs.append((half.at[rows(lax.rem(x + k, 4) * q, q), left], r1.at[0, k - 1], over_x[k - 1]))
        jobs.append((half.at[rows(lax.rem(z + k, 4) * q, q), right], r1.at[1, k - 1], over_z[k - 1]))
    send.run(jobs)
    quarter[0] = (half[rows(x * q, q), left] + r1[0, 1]) + (r1[0, 0] + r1[0, 2])
    quarter[1] = (half[rows(z * q, q), right] + r1[1, 1]) + (r1[1, 0] + r1[1, 2])
    jobs = []
    for k in (2, 1, 3):
        jobs.append((quarter.at[0, rows(lax.rem(z + k, 4) * s, s)], r2.at[0, k - 1], over_z[k - 1]))
        jobs.append((quarter.at[1, rows(lax.rem(x + k, 4) * s, s)], r2.at[1, k - 1], over_x[k - 1]))
    send.run(jobs)
    ry[y, 0] = (quarter[0, rows(z * s, s), :] + r2[0, 1]) + (r2[0, 0] + r2[0, 2])
    ry[y, 1] = (quarter[1, rows(x * s, s), :] + r2[1, 1]) + (r2[1, 0] + r2[1, 2])
    for k in (0, 1, 2):
        slot = ry.at[lax.rem(y + k, 4)]
        copy = send.start(slot, slot, down)
        if k == 2:
            behind()
        copy.wait()


def put_piece(out_ref, block, ry, slots):
    z, x, y, core = place()
    n = out_ref.shape[1]
    h, q, s, w = n // 2, n // 8, n // 32, n // 2
    at = (core * h + x * q + z * s, core * h + z * q + x * s)
    for side in (0, 1):
        total = ry[slots[0], side] + ry[slots[1], side]
        for i in range(2, len(slots), 2):
            total = total + (ry[slots[i], side] + ry[slots[i + 1], side])
        out_ref[block, rows(at[side], s), pl.ds(side * w, w)] = total


def gather_rows(send, where, out_ref):
    over_core, over_x, over_z, down = where
    z, x, y, core = place()
    n = out_ref.shape[1]
    h, q, s, w = n // 2, n // 8, n // 32, n // 2
    left, right = pl.ds(0, w), pl.ds(w, w)
    lpart = out_ref.at[:, rows(core * h + x * q + z * s, s), left]
    rpart = out_ref.at[:, rows(core * h + z * q + x * s, s), right]
    jobs = []
    for k in (2, 1, 3):
        jobs += [(lpart, lpart, over_z[k - 1]), (rpart, rpart, over_x[k - 1])]
    send.run(jobs)
    block = (
        lambda k: out_ref.at[:, rows(core * h + lax.rem(x + k, 4) * q, q), left],
        lambda k: out_ref.at[:, rows(core * h + lax.rem(z + k, 4) * q, q), right],
    )
    landing = []
    for k in (1, 3, 2):
        for side, over in ((0, over_x), (1, over_z)):
            landing.append((send.start(block[side](0), block[side](0), over[k - 1]), side, k))
    passing = [send.start(block[side](0), block[side](0), over_core[0]) for side in (0, 1)]
    for copy, side, k in landing:
        copy.wait_recv()
        part = block[side](4 - k)
        passing.append(send.start(part, part, over_core[0]))
    for copy, _, _ in landing:
        copy.wait_send()
    for copy in passing:
        copy.wait()


def split(x):
    high = x.astype(jnp.bfloat16)
    return high, (x - high.astype(jnp.float32)).astype(jnp.bfloat16)


def dot4(a, b, over):
    dims = ((over[:1], over[1:]), ((), ()))
    dot = lambda l, r: lax.dot_general(l, r, dims, preferred_element_type=jnp.float32)
    return dot(a[0], b[0]) + (dot(a[0], b[1]) + (dot(a[1], b[0]) + dot(a[1], b[1])))


CHUNK = 256
EARLY = 2
PART = CHUNK // 4
CROSS = 8 * CHUNK + PART
LEFT = 2
ROUND = 2


def dot_tn(a, b):
    return lax.dot_general(a, b, (((0,), (0,)), ((), ())), preferred_element_type=jnp.float32)


def thrice(x):
    high, low = split(x)
    return [high, high, low]


def weights(x):
    high, low = split(x)
    return jnp.concatenate([high, low, high], axis=1)


def whole_kernel(root, x_ref, own, factor_ref, got, w, relay, grams, la, xa, cross, lba, lb, xb, xba, acc,
                 half, quarter, rc, r1, r2, ry, half_b, quarter_b, rc_b, r1_b, r2_b, ry_b,
                 load_sem, go_sem, come_sem, hop_go_sem, hop_come_sem, send_sem, recv_sem):
    send = Sender(send_sem, recv_sem)
    snap = lax.axis_index("snap")
    first, second = snap == 0, snap == 1
    other = (lax.axis_index("dof"), 1 - snap)
    count, n = x_ref.shape
    chunks = count // CHUNK
    paired = chunks // 2
    direct = chunks - ROUND
    chunk = lambda c: pl.ds(pl.multiple_of(c * CHUNK, CHUNK), CHUNK)
    pair = lambda c: pl.ds(pl.multiple_of(c * 2 * CHUNK, 2 * CHUNK), 2 * CHUNK)

    def stream(c, base):
        return pltpu.make_async_remote_copy(
            src_ref=x_ref.at[pl.ds(pl.multiple_of(c * CHUNK + base, PART), CHUNK)], dst_ref=got.at[chunk(c)],
            send_sem=go_sem.at[c], recv_sem=come_sem.at[c], device_id=other, device_id_type=MESH)

    def stream_part(start, base, size, sem):
        return pltpu.make_async_remote_copy(
            src_ref=x_ref.at[pl.ds(start + base, size)], dst_ref=got.at[pl.ds(start, size)],
            send_sem=go_sem.at[sem], recv_sem=come_sem.at[sem], device_id=other, device_id_type=MESH)

    a_parts = [stream_part(paired * CHUNK, 0, PART, paired), stream_part(CROSS, 0, CHUNK - PART, chunks)]
    last_b = stream_part((paired - 1) * CHUNK, CROSS, CHUNK - PART, paired - 1)

    def loop(begin, end, body):
        def step(c, carry):
            body(c)
            return carry

        lax.fori_loop(begin, end, step, 0)

    load = lambda c: pltpu.make_async_copy(x_ref.at[chunk(c)], own.at[chunk(c)], load_sem.at[c])
    loop(0, chunks, lambda c: load(c).start())
    where = neighbours(True)
    down = where[3]

    def hop(which, i):
        src = (x_ref.at[chunk(direct + i)], relay.at[i], relay.at[i])[which]
        dst = (relay.at[i], relay.at[i], got.at[chunk(direct + i)])[which]
        go = hop_go_sem.at[i if which < 2 else ROUND + i]
        come = hop_come_sem.at[i] if which < 2 else come_sem.at[direct + i]
        return pltpu.make_async_remote_copy(
            src_ref=src, dst_ref=dst, send_sem=go, recv_sem=come, device_id=down, device_id_type=MESH)

    @pl.when(first)
    def _():
        loop(0, paired, lambda c: stream(c, 0).start())
        for copy in a_parts:
            copy.start()
        loop(paired + 1, direct, lambda c: stream(c, 0).start())

    @pl.when(second)
    def _():
        loop(0, EARLY, lambda c: stream(c, CROSS).start())
        last_b.start()

    acc[...] = jnp.zeros_like(acc)

    def gram_one(c):
        load(c).wait()
        high, low = split(own[chunk(c), :])
        half_high, half_low = high * jnp.bfloat16(0.5), low * jnp.bfloat16(0.5)
        acc[...] += dot_tn(high, half_high) + dot_tn(high, low) + dot_tn(low, half_low)

    loop(0, chunks, gram_one)
    acc[...] = acc[...] + acc[...].T

    def behind_first():
        @pl.when(second)
        def _():
            loop(EARLY, paired - 1, lambda c: stream(c, CROSS).start())

        @pl.when(first)
        def _():
            for i in range(ROUND):
                hop(0, i).start()

    scatter_sum(send, where, acc, half, quarter, rc, r1, r2, ry, behind_first)
    put_piece(grams, 0, ry, (0, 2))
    put_piece(grams, 1, ry, (1, 3))
    gather_rows(send, where, grams)
    acc[...] = grams[0]
    factor_into(acc, la, xa, n)

    def basis_one(c, values, width):
        own[pair(c), :] = lax.dot_general(
            jnp.concatenate(values, axis=1), w[:, :width], (((1,), (1,)), ((), ())),
            preferred_element_type=jnp.float32)

    @pl.when(first)
    def _():
        w[:, :3 * n] = weights(xa[...] * root)
        factor_ref[:n, :] = la[...].T / root
        factor_ref[n:, :] = jnp.zeros((n, n), jnp.float32)

    acc[...] = jnp.zeros_like(acc)

    def add_cross(start, size, own_start):
        there = got[pl.ds(start, size), :]
        here = own[pl.ds(own_start, size), :]
        left = split(jnp.where(second, here, there))
        right = split(jnp.where(second, there, here))
        acc[...] += dot4(left, right, (0, 0))

    @pl.when(second)
    def _():
        hop(0, 0).wait_recv()
        hop(1, 0).start()

    def cross_one(c):
        stream(c, 0).wait_recv()
        start = pl.multiple_of(c * CHUNK, CHUNK)
        add_cross(start, CHUNK, pl.multiple_of(start + (1 - snap) * CROSS, PART))

    loop(0, paired - 1, cross_one)
    tail = (paired - 1) * CHUNK

    @pl.when(first)
    def _():
        last_b.wait_recv()
        add_cross(tail, CHUNK - PART, tail + CROSS)

    @pl.when(second)
    def _():
        stream(paired - 1, 0).wait_recv()
        add_cross(tail, CHUNK, tail)
        a_parts[0].wait_recv()
        add_cross(paired * CHUNK, PART, paired * CHUNK)

    scatter_sum(send, where, acc, half_b, quarter_b, rc_b, r1_b, r2_b, ry_b, lambda: None)
    put_piece(cross, 0, ry_b, (0, 2, 1, 3))
    @pl.when(second)
    def _():
        for i in range(1, ROUND):
            hop(0, i).wait_recv()
            hop(1, i).start()

    @pl.when(first)
    def _():
        hop(1, 0).wait_recv()
        hop(2, 0).start()

    gather_rows(send, where, cross)

    @pl.when(first)
    def _():
        for i in range(1, ROUND):
            hop(1, i).wait_recv()
            hop(2, i).start()

    @pl.when(second)
    def _():
        lba[...] = dot_nt(cross[0], xa[...])
        acc[...] = grams[1] - dot_nt(lba[...], lba[...])
        factor_into(acc, lb, xb, n)
        xba[...] = -dot_nn(xb[...], dot_nn(lba[...], xa[...]))
        w[:, :3 * n] = weights(xb[...] * root)
        w[:, 3 * n:] = weights(xba[...] * root)
        factor_ref[:n, :] = lba[...].T / root
        factor_ref[n:, :] = lb[...].T / root

        def one(c):
            @pl.when(c > paired // 2)
            def _():
                stream(2 * c, 0).wait_recv()

            @pl.when(c >= paired // 2)
            def _():
                stream(2 * c + 1, 0).wait_recv()

            basis_one(c, thrice(own[pair(c), :]) + thrice(got[pair(c), :]), 6 * n)

        a_parts[1].wait_recv()
        loop(0, paired - LEFT, one)
        for c in range(2 * (paired - LEFT), chunks):
            stream(c, 0).wait_recv()
        loop(0, paired - 1, lambda c: stream(c, CROSS).wait_send())
        last_b.wait_send()
        for i in range(ROUND):
            hop(1, i).wait_send()

    @pl.when(first)
    def _():
        loop(0, paired - LEFT, lambda c: basis_one(c, thrice(own[pair(c), :]), 3 * n))
        loop(0, paired, lambda c: stream(c, 0).wait_send())
        for copy in a_parts:
            copy.wait_send()
        loop(paired + 1, direct, lambda c: stream(c, 0).wait_send())
        for i in range(ROUND):
            hop(0, i).wait_send()
            hop(2, i).wait_send()


def whole(snapshots, root):
    count, n = snapshots.shape
    chunks = count // CHUNK
    f32 = jnp.float32
    sums = [
        pltpu.VMEM((n // 2, n), f32),
        pltpu.VMEM((2, n // 8, n // 2), f32),
        pltpu.VMEM((n // 2, n), f32),
        pltpu.VMEM((2, 3, n // 8, n // 2), f32),
        pltpu.VMEM((2, 3, n // 32, n // 2), f32),
        pltpu.VMEM((4, 2, n // 32, n // 2), f32),
    ]
    square = pltpu.VMEM((n, n), f32)
    dma = pltpu.SemaphoreType.DMA
    return pl.pallas_call(
        functools.partial(whole_kernel, root),
        out_shape=(jax.ShapeDtypeStruct((count, n), f32), jax.ShapeDtypeStruct((2 * n, n), f32),
                   jax.ShapeDtypeStruct((count, n), f32), jax.ShapeDtypeStruct((n, 6 * n), jnp.bfloat16)),
        in_specs=[pl.BlockSpec(memory_space=pl.ANY)],
        out_specs=(VMEM,) * 4,
        scratch_shapes=[pltpu.VMEM((ROUND, CHUNK, n), f32)]
        + [pltpu.VMEM((2, n, n), f32), square, square, pltpu.VMEM((1, n, n), f32)] + [square] * 5
        + sums + sums
        + [dma((chunks,)), dma((chunks + 1,)), dma((chunks + 1,)), dma((2 * ROUND,)), dma((ROUND,)), dma((72,)), dma((72,))],
        compiler_params=pltpu.CompilerParams(
            collective_id=0, has_side_effects=True, vmem_limit_bytes=30 << 20),
        cost_estimate=pl.CostEstimate(flops=130 << 30, bytes_accessed=400 << 20, transcendentals=0),
    )(snapshots)


def finish_kernel(own, factor, got, w, basis_out, factor_out, stage, sems):
    count, n = own.shape
    size = 2 * CHUNK
    done = count - LEFT * size
    second = lax.axis_index("snap") == 1
    copies = [
        pltpu.make_async_copy(own.at[pl.ds(0, done)], basis_out.at[pl.ds(0, done)], sems.at[0]),
        pltpu.make_async_copy(factor, factor_out, sems.at[1]),
    ]
    for copy in copies:
        copy.start()
    for i in range(LEFT):
        at = pl.ds(done + i * size, size)

        def make(values, width):
            stage[i] = lax.dot_general(
                jnp.concatenate(values, axis=1), w[:, :width], (((1,), (1,)), ((), ())),
                preferred_element_type=jnp.float32)

        @pl.when(second)
        def _():
            make(thrice(own[at, :]) + thrice(got[at, :]), 6 * n)

        @pl.when(jnp.logical_not(second))
        def _():
            make(thrice(own[at, :]), 3 * n)

        copies.append(pltpu.make_async_copy(stage.at[i], basis_out.at[at], sems.at[2 + i]))
        copies[-1].start()
    for copy in copies:
        copy.wait()


def finish(own, factor, got, w):
    count, n = own.shape
    here = pl.BlockSpec(memory_space=pl.ANY)
    return pl.pallas_call(
        finish_kernel,
        out_shape=(jax.ShapeDtypeStruct(own.shape, own.dtype), jax.ShapeDtypeStruct(factor.shape, factor.dtype)),
        in_specs=[VMEM] * 4,
        out_specs=(here, here),
        scratch_shapes=[pltpu.VMEM((LEFT, 2 * CHUNK, n), jnp.float32), pltpu.SemaphoreType.DMA((2 + LEFT,))],
        compiler_params=pltpu.CompilerParams(vmem_limit_bytes=30 << 20),
    )(own, factor, got, w)


def on_device(snapshots):
    root_rows = float(snapshots.shape[0] * lax.axis_size("dof")) ** 0.5
    return tuple(finish(*whole(snapshots, root_rows)))


def solution(mesh):
    in_specs = (P("dof", "snap"),)
    out_specs = (P("dof", "snap"), P(None, "snap"))
    return jax.shard_map(
        on_device, mesh=mesh, in_specs=in_specs, out_specs=out_specs, check_vma=False
    )
```
